512 devices in a mesh: blk: 16 (over y, z_lo), wide: 32 (over x, z_hi, core).
Axes of the slice: x: 4, y: 8, z: 8 (z_hi: 4, z_lo: 2; z = z_hi * 2 + z_lo), core: 2. Of those that a mesh axis runs over, the one named last changes fastest.
Arguments:
- tokens: bfloat16 [24576, 128], P(('blk', 'wide')), may hold values from -11 to 11
- centroids: bfloat16 [131072, 128], P('blk'), may hold values from -7 to 7
- row_ids: int32 [512, 16, 32], P(('blk', 'wide')), may hold values from 0 to 47
- alt_ids: int32 [512, 16, 32], P(('blk', 'wide')), may hold values from 0 to 8191
- counts: int32 [512, 16], P(('blk', 'wide')), may hold values from 1 to 32, as said below
Outputs:
- row_duals: float32 [24576], P(('blk', 'wide'))
- col_duals: float32 [131072], P('blk')
- residuals: float32 [512, 16, 32, 128], P(('blk', 'wide'))
The draws below stay inside these ranges and needn't reach their ends.
Inputs may be any that keep to these rules, and one draw needn't show every extreme that they name: `row_ids`: slot (d, b, c) names row d * 48 + value. `alt_ids`: slot (d, b, c) names centroid b * 8192 + value. The first counts[d, b] slots of device d toward owner b are live; one owner, the same on every device, gets 32 live slots from every device.
All inputs are finite; a program needn't handle non-finite values.
Results may differ from the reference program's by a relative error of at most 0.0003.
Values may be sent and summed in bfloat16 or wider, within the bound.
No kernel may reach another device: no remote copies, remote signals or barrier semaphores. Data moves between devices by JAX's collectives and lax.ppermute only.
A program may use at most 64 MiB of HBM per device.

```python
import math
import jax
import jax.numpy as jnp
from jax import lax

D = 128
SLAB = 8192
CAP = 32
TOK_DEV = 48
K = 131072
TOKENS = 24576
N_BLK = 16
DEVICES = 512


def draw_centroids(key, part):
    inner = jax.random.fold_in(key, 1)
    values = jnp.clip(jax.random.normal(inner, (K, D), jnp.float32), -6.0, 6.0)
    return values.astype(jnp.bfloat16)


def draw_tokens(key, part):
    inner = jax.random.fold_in(key, 3)
    values = jnp.clip(jax.random.normal(inner, (TOKENS, D), jnp.float32), -6.0, 6.0)
    return values.astype(jnp.bfloat16)


def draw_counts(key, part):
    busiest = jax.random.randint(jax.random.fold_in(key, 5), (), 0, N_BLK)
    others = jax.random.randint(jax.random.fold_in(key, 6), (DEVICES, N_BLK), 1, CAP // 2 + 1)
    owners = jnp.arange(N_BLK)[None, :]
    return jnp.where(owners == busiest, CAP, others).astype(jnp.int32)


def set_ends(values, stream_key, smallest, top_value):
    index_at = [jax.random.randint(jax.random.fold_in(stream_key, axis), (), 0, length) for axis, length in enumerate(values.shape)]
    widest = values.shape.index(max(values.shape))
    beside = index_at[:widest] + [(index_at[widest] + 1) % values.shape[widest]] + index_at[widest + 1:]
    return values.at[tuple(index_at)].set(smallest).at[tuple(beside)].set(top_value)


def setup_inputs(seed: int = 0) -> dict:
    streams_of = jax.random.split(jax.random.key(seed), 6)
    tokens = draw_tokens(jax.random.fold_in(streams_of[5], 71), 0)
    centroids = draw_centroids(jax.random.fold_in(streams_of[5], 71), 0)
    row_ids = set_ends(jax.random.randint(streams_of[2], (DEVICES, N_BLK, CAP), 0, TOK_DEV), jax.random.fold_in(streams_of[2], 1), 0, TOK_DEV - 1).astype(jnp.int32)
    alt_ids = set_ends(jax.random.randint(streams_of[3], (DEVICES, N_BLK, CAP), 0, SLAB), jax.random.fold_in(streams_of[3], 1), 0, SLAB - 1).astype(jnp.int32)
    counts = draw_counts(jax.random.fold_in(streams_of[5], 71), 0)
    return dict(tokens=tokens, centroids=centroids, row_ids=row_ids, alt_ids=alt_ids, counts=counts)


score_gain = 3.0

def reference(tokens, centroids, row_ids, alt_ids, counts):
    scaling = score_gain / math.sqrt(D)
    token_rows = tokens.astype(jnp.float32)
    centre_rows = centroids.astype(jnp.float32)
    block_rows = math.gcd(TOKENS, 512)
    blocks = token_rows.reshape(TOKENS // block_rows, block_rows, D)

    def scores_of(rows_block):
        return jnp.dot(rows_block, centre_rows.T, precision=lax.Precision.HIGHEST) * scaling

    def row_total(rows_block):
        scores = scores_of(rows_block)
        peak_score = lax.optimization_barrier(jnp.max(scores, axis=1))
        return peak_score + jnp.log(lax.optimization_barrier(jnp.sum(jnp.exp(scores - peak_score[:, None]), axis=1)))
    log_totals = lax.map(row_total, blocks).reshape(TOKENS)
    row_duals = math.log(K) - log_totals
    dual_blocks = row_duals.reshape(TOKENS // block_rows, block_rows)

    def add_mass(carry, paired):
        rows_block, duals_block = paired
        scores = scores_of(rows_block)
        return (carry + lax.optimization_barrier(jnp.sum(jnp.exp(scores + duals_block[:, None]), axis=0)), None)
    masses, unused = lax.scan(add_mass, jnp.zeros((K,), jnp.float32), (blocks, dual_blocks))
    col_duals = math.log(TOKENS) - jnp.log(masses)
    device_rows = jnp.arange(DEVICES, dtype=jnp.int32)[:, None, None] * TOK_DEV + row_ids.astype(jnp.int32)
    owner_cols = jnp.arange(N_BLK, dtype=jnp.int32)[None, :, None] * SLAB + alt_ids.astype(jnp.int32)
    flat_rows = device_rows.reshape(-1)
    flat_cols = owner_cols.reshape(-1)
    picked = token_rows[flat_rows]
    centres = centre_rows[flat_cols]
    pair_scores = lax.optimization_barrier(jnp.sum(picked * centres, axis=1)) * scaling
    weights = jnp.exp(pair_scores + row_duals[flat_rows] + col_duals[flat_cols])
    live = (jnp.arange(CAP, dtype=jnp.int32)[None, None, :] < counts[:, :, None]).reshape(-1)
    weights = jnp.where(live, weights, jnp.zeros_like(weights))
    residuals = (weights[:, None] * (picked - centres)).reshape(DEVICES, N_BLK, CAP, D)
    return (row_duals, col_duals, residuals)
```

```python
import math

import jax
import jax.numpy as jnp
from jax import lax
from jax.experimental import pallas as pl
from jax.experimental.pallas import tpu as pltpu
from jax.sharding import PartitionSpec as P

score_gain = 3.0
log2e = 1.4426950408889634
dead = -1.0e30


def vmem(n):
    return [pl.BlockSpec(memory_space=pltpu.VMEM)] * n


def load_rows(x_ref, t_ref, n_blk, tok):
    for i in range(n_blk):
        t_ref[i * tok : (i + 1) * tok, :] = x_ref[i, :tok, :]


def exchange(x, axis):
    return lax.all_to_all(x, axis, split_axis=0, concat_axis=0, tiled=True)


def row_pass(x, centroids, tok, scaling):
    n_blk = x.shape[0]
    rows = n_blk * tok
    slab, width = centroids.shape
    block = 256
    steps = slab // block
    factor = scaling * log2e

    def kernel(x_ref, c_ref, out_ref, t_ref, s_ref, m_ref, a_ref):
        load_rows(x_ref, t_ref, n_blk, tok)

        def scores(j):
            return lax.dot_general(
                c_ref[pl.ds(pl.multiple_of(j * block, block), block), :],
                t_ref[...],
                (((1,), (1,)), ((), ())),
                preferred_element_type=jnp.float32,
            )

        m_ref[...] = jnp.full_like(m_ref, dead)
        a_ref[...] = jnp.zeros_like(a_ref)
        s_ref[0] = scores(0)

        def step(j, carry):
            now = lax.rem(j, 2)
            s_ref[1 - now] = scores(jnp.minimum(j + 1, steps - 1))
            for g in range(rows // 128):
                lanes = slice(g * 128, (g + 1) * 128)
                s = s_ref[now, :, lanes].reshape(block // 8, 8, 128)
                old = m_ref[:, lanes]
                new = jnp.maximum(old, jnp.max(s, axis=0))
                m_ref[:, lanes] = new
                part = jnp.sum(jnp.exp2((s - new[None]) * factor), axis=0)
                a_ref[:, lanes] = a_ref[:, lanes] * jnp.exp2((old - new) * factor) + part
            return carry

        lax.fori_loop(0, steps, step, 0)
        m = m_ref[...]
        top = jnp.max(m, axis=0, keepdims=True)
        total = jnp.sum(a_ref[...] * jnp.exp2((m - top) * factor), axis=0, keepdims=True)
        lse = top * scaling + jnp.log(total)
        for i in range(n_blk):
            out_ref[i] = lse

    return pl.pallas_call(
        kernel,
        out_shape=jax.ShapeDtypeStruct((n_blk, 1, rows), jnp.float32),
        in_specs=vmem(2),
        out_specs=pl.BlockSpec(memory_space=pltpu.VMEM),
        scratch_shapes=[
            pltpu.VMEM((rows, width), jnp.bfloat16),
            pltpu.VMEM((2, block, rows), jnp.float32),
            pltpu.VMEM((8, rows), jnp.float32),
            pltpu.VMEM((8, rows), jnp.float32),
        ],
        compiler_params=pltpu.CompilerParams(vmem_limit_bytes=24 << 20),
        name="row_pass",
    )(x, centroids)


def column_pass(x, centroids, parts, tok, scaling, all_cols, chunks):
    n_blk = x.shape[0]
    rows = n_blk * tok
    slab, width = centroids.shape
    block = slab // chunks
    factor = scaling * log2e

    def kernel(x_ref, c_ref, l_ref, dual_ref, mass_ref, t_ref, d_ref, s_ref):
        load_rows(x_ref, t_ref, n_blk, tok)
        lse = l_ref[:, 0, :]
        top = jnp.max(lse, axis=0, keepdims=True)
        total = jnp.sum(jnp.exp(lse - top), axis=0, keepdims=True)
        dual = math.log(all_cols) - (top + jnp.log(total))
        dual_ref[...] = dual
        d_ref[...] = jnp.transpose(jnp.broadcast_to(dual * log2e, (128, rows)))

        def scores(j):
            return lax.dot_general(
                t_ref[...],
                c_ref[pl.ds(pl.multiple_of(j * block, block), block), :],
                (((1,), (1,)), ((), ())),
                preferred_element_type=jnp.float32,
            )

        s_ref[0] = scores(0)

        def step(j, carry):
            now = lax.rem(j, 2)
            s_ref[1 - now] = scores(jnp.minimum(j + 1, chunks - 1))
            for g in range(block // 128):
                lanes = slice(g * 128, (g + 1) * 128)
                acc = jnp.zeros((8, 128), jnp.float32)
                for r in range(0, rows, 128):
                    s = s_ref[now, r : r + 128, lanes]
                    e = jnp.exp2(s * factor + d_ref[r : r + 128, :])
                    acc = acc + jnp.sum(e.reshape(16, 8, 128), axis=0)
                mass_ref[j, :, lanes] = jnp.sum(acc, axis=0, keepdims=True)
            return carry

        lax.fori_loop(0, chunks, step, 0)

    return pl.pallas_call(
        kernel,
        out_shape=(
            jax.ShapeDtypeStruct((1, rows), jnp.float32),
            jax.ShapeDtypeStruct((chunks, 1, block), jnp.float32),
        ),
        in_specs=vmem(3),
        out_specs=tuple(vmem(2)),
        scratch_shapes=[
            pltpu.VMEM((rows, width), jnp.bfloat16),
            pltpu.VMEM((rows, 128), jnp.float32),
            pltpu.VMEM((2, rows, block), jnp.float32),
        ],
        compiler_params=pltpu.CompilerParams(vmem_limit_bytes=24 << 20),
        name="column_pass",
    )(x, centroids, parts)


def sum_and_copy(parts):
    def kernel(p_ref, out_ref):
        total = jnp.sum(p_ref[:, 0, :], axis=0, keepdims=True)
        for j in range(parts.shape[0]):
            out_ref[j] = total

    return pl.pallas_call(
        kernel,
        out_shape=jax.ShapeDtypeStruct(parts.shape, jnp.float32),
        in_specs=vmem(1),
        out_specs=pl.BlockSpec(memory_space=pltpu.VMEM),
        name="sum_and_copy",
    )(parts)


def look_up(masses, high, low, all_rows, n_blk, capacity):
    chunks, _, block = masses.shape
    lines = chunks * block // 128
    slots = high.shape[1]

    def kernel(m_ref, h_ref, l_ref, dual_ref, out_ref):
        for j in range(chunks):
            for g in range(block // 128):
                k = j * (block // 128) + g
                dual_ref[k : k + 1, :] = m_ref[j, :, g * 128 : (g + 1) * 128]
        dual = math.log(all_rows) - jnp.log(dual_ref[...])
        dual_ref[...] = dual
        line = lax.broadcasted_iota(jnp.int32, (lines, slots), 0)
        pick = jnp.where(line == h_ref[...], 1.0, 0.0).astype(jnp.bfloat16)
        rest = dual
        found = jnp.zeros((128, slots), jnp.float32)
        for _ in range(3):
            piece = rest.astype(jnp.bfloat16)
            rest = rest - piece.astype(jnp.float32)
            found = found + lax.dot_general(
                piece, pick, (((0,), (0,)), ((), ())), preferred_element_type=jnp.float32
            )
        lane = lax.broadcasted_iota(jnp.int32, (128, slots), 0)
        value = jnp.sum(jnp.where(lane == l_ref[...], found, 0.0), axis=0, keepdims=True)
        out_ref[...] = jnp.zeros_like(out_ref)
        for i in range(n_blk):
            out_ref[i, :, :capacity] = value[:, i * capacity : (i + 1) * capacity]

    return pl.pallas_call(
        kernel,
        out_shape=(
            jax.ShapeDtypeStruct((lines, 128), jnp.float32),
            jax.ShapeDtypeStruct((n_blk, 1, 128), jnp.float32),
        ),
        in_specs=vmem(3),
        out_specs=tuple(vmem(2)),
        name="look_up",
    )(masses, high, low)


def prepare(tokens, centres, rows, live, duals, scaling):
    slots, width = rows.shape[0], tokens.shape[1]
    tok = tokens.shape[0]

    def kernel(t_ref, c_ref, r_ref, v_ref, d_ref, diff_ref, exp_ref):
        row = lax.broadcasted_iota(jnp.int32, (slots, tok), 1)
        hit = row == r_ref[...]
        picked = jnp.dot(
            jnp.where(hit, 1.0, 0.0).astype(jnp.bfloat16), t_ref[...], preferred_element_type=jnp.float32
        )
        centre = c_ref[...].astype(jnp.float32)
        diff_ref[...] = picked - centre
        score = jnp.sum(picked * centre, axis=1, keepdims=True) * scaling
        dual = jnp.sum(jnp.where(hit, d_ref[...], 0.0), axis=1, keepdims=True)
        exponent = jnp.where(v_ref[...] > 0, score + dual, dead)
        exp_ref[...] = jnp.broadcast_to(exponent, (slots, width))

    shape = jax.ShapeDtypeStruct((slots, width), jnp.float32)
    return pl.pallas_call(
        kernel,
        out_shape=(shape, shape),
        in_specs=vmem(5),
        out_specs=tuple(vmem(2)),
        name="prepare",
    )(tokens, centres, rows, live, duals)


def finish(duals, diff, exponents, n_blk, capacity):
    width = diff.shape[1]

    def kernel(g_ref, d_ref, e_ref, out_ref):
        turned = jnp.transpose(g_ref[:, 0, :])
        for i in range(n_blk):
            part = slice(i * capacity, (i + 1) * capacity)
            dual = jnp.broadcast_to(turned[:capacity, i : i + 1], (capacity, width))
            e = e_ref[part, :]
            weight = jnp.where(e > 0.1 * dead, jnp.exp(e + dual), 0.0)
            out_ref[0, i] = weight * d_ref[part, :]

    return pl.pallas_call(
        kernel,
        out_shape=jax.ShapeDtypeStruct((1, n_blk, capacity, width), jnp.float32),
        in_specs=vmem(3),
        out_specs=pl.BlockSpec(memory_space=pltpu.VMEM),
        name="finish",
    )(duals, diff, exponents)


def local(tokens, centroids, row_ids, alt_ids, counts):
    tok, width = tokens.shape
    slab = centroids.shape[0]
    n_blk = lax.axis_size("blk")
    n_wide = lax.axis_size("wide")
    position = lax.axis_index("blk")
    scaling = score_gain / math.sqrt(width)
    capacity = alt_ids.shape[2]
    slots = n_blk * capacity

    ids = alt_ids[0]
    line = jnp.concatenate([ids >> 7, ids & 127], axis=1).astype(jnp.bfloat16)
    line = jnp.pad(line, ((0, 0), (0, width - 2 * capacity)))[:, None, :]
    outgoing = jnp.concatenate([jnp.broadcast_to(tokens[None], (n_blk, tok, width)), line], axis=1)
    gathered = exchange(outgoing, "blk")

    parts = exchange(row_pass(gathered, centroids, tok, scaling), "blk")

    asked = gathered[:, tok, :].astype(jnp.int32)
    high = asked[:, :capacity].reshape(1, slots)
    low = asked[:, capacity : 2 * capacity].reshape(1, slots)
    wanted = (high * 128 + low).reshape(slots)
    centres = exchange(centroids[wanted].reshape(n_blk, capacity, width), "blk")
    centres = centres.reshape(slots, width)

    duals, partial_mass = column_pass(gathered, centroids, parts, tok, scaling, slab * n_blk, n_wide)
    own_duals = lax.dynamic_slice_in_dim(duals[0], position * tok, tok)

    chunk = sum_and_copy(exchange(partial_mass, "wide"))
    masses = exchange(chunk, "wide")
    col_duals, found = look_up(masses, high, low, tok * n_blk * n_wide, n_blk, capacity)
    found = exchange(found, "blk")

    live = (jnp.arange(capacity, dtype=jnp.int32)[None, :] < counts[0][:, None]).astype(jnp.int32)
    diff, exponents = prepare(
        tokens, centres, row_ids.reshape(slots, 1), live.reshape(slots, 1), own_duals[None, :], scaling
    )
    residuals = finish(found, diff, exponents, n_blk, capacity)
    return (own_duals, col_duals.reshape(slab), residuals)


def solution(mesh):
    in_specs = (
        P(("blk", "wide"), None),
        P("blk", None),
        P(("blk", "wide"), None, None),
        P(("blk", "wide"), None, None),
        P(("blk", "wide"), None),
    )
    out_specs = (P(("blk", "wide")), P("blk"), P(("blk", "wide"), None, None, None))
    return jax.shard_map(local, mesh=mesh, in_specs=in_specs, out_specs=out_specs, check_vma=False)
```

```python
import math

import jax
import jax.numpy as jnp
from jax import lax
from jax.experimental import pallas as pl
from jax.experimental.pallas import tpu as pltpu
from jax.sharding import PartitionSpec as P

score_gain = 3.0
log2e = 1.4426950408889634
dead = -1.0e30


def vmem(n):
    return [pl.BlockSpec(memory_space=pltpu.VMEM)] * n


def load_rows(x_ref, t_ref, n_blk, tok):
    for i in range(n_blk):
        t_ref[i * tok : (i + 1) * tok, :] = x_ref[i, :tok, :]


def exchange(x, axis):
    return lax.all_to_all(x, axis, split_axis=0, concat_axis=0, tiled=True)


def params(mib):
    return pltpu.CompilerParams(vmem_limit_bytes=mib << 20)


def pack(tokens, alt_ids):
    tok, width = tokens.shape
    n_blk, capacity = alt_ids.shape

    def kernel(t_ref, a_ref, out_ref):
        ids = a_ref[...]
        line = jnp.concatenate(
            [ids >> 7, ids & 127, jnp.zeros((n_blk, width - 2 * capacity), jnp.int32)], axis=1
        ).astype(jnp.float32)
        rows = t_ref[...]
        for i in range(n_blk):
            out_ref[i, :tok, :] = rows
            out_ref[i, tok:, :] = line[i : i + 1, :].astype(jnp.bfloat16)

    return pl.pallas_call(
        kernel,
        out_shape=jax.ShapeDtypeStruct((n_blk, tok + 1, width), jnp.bfloat16),
        in_specs=vmem(2),
        out_specs=pl.BlockSpec(memory_space=pltpu.VMEM),
        compiler_params=params(4),
        name="pack",
    )(tokens, alt_ids)


def row_pass(x, centroids, tok, capacity, scaling):
    n_blk = x.shape[0]
    rows = n_blk * tok
    slots = n_blk * capacity
    slab, width = centroids.shape
    factor = scaling * log2e
    block = math.gcd(slab, 2048)
    small = math.gcd(slab, 256)

    def kernel(x_ref, c_ref, out_ref, ids_ref, t_ref, m_ref, a_ref):
        load_rows(x_ref, t_ref, n_blk, tok)
        for i in range(n_blk):
            line = x_ref[i, tok:, :].astype(jnp.float32).astype(jnp.int32)
            part = slice(i * capacity, (i + 1) * capacity)
            ids_ref[0:1, part] = line[:, :capacity]
            ids_ref[1:2, part] = line[:, capacity : 2 * capacity]
            ids_ref[2:3, part] = line[:, :capacity] * 128 + line[:, capacity : 2 * capacity]

        def scores(start, size, lanes):
            return lax.dot_general(
                c_ref[pl.ds(start, size), :],
                t_ref[lanes, :],
                (((1,), (1,)), ((), ())),
                preferred_element_type=jnp.float32,
            ).reshape(size // 8, 8, 256)

        def rescale_free():
            for g in range(rows // 256):
                lanes = slice(g * 256, (g + 1) * 256)
                first = jnp.max(scores(0, small, lanes), axis=(0, 1)).reshape(1, 256)
                m_ref[:, lanes] = jnp.broadcast_to(first, (8, 256))
            a_ref[...] = jnp.zeros_like(a_ref)

            def step(j, carry):
                start = pl.multiple_of(j * block, block)
                for g in range(rows // 256):
                    lanes = slice(g * 256, (g + 1) * 256)
                    e = jnp.exp2((scores(start, block, lanes) - m_ref[:, lanes][None]) * factor)
                    a_ref[:, lanes] = a_ref[:, lanes] + jnp.sum(e, axis=0)
                return carry

            lax.fori_loop(0, slab // block, step, 0)

        def rescaled():
            m_ref[...] = jnp.full_like(m_ref, dead)
            a_ref[...] = jnp.zeros_like(a_ref)

            def step(j, carry):
                start = pl.multiple_of(j * small, small)
                for g in range(rows // 256):
                    lanes = slice(g * 256, (g + 1) * 256)
                    s = scores(start, small, lanes)
                    old = m_ref[:, lanes]
                    new = jnp.maximum(old, jnp.max(s, axis=0))
                    m_ref[:, lanes] = new
                    part = jnp.sum(jnp.exp2((s - new[None]) * factor), axis=0)
                    a_ref[:, lanes] = a_ref[:, lanes] * jnp.exp2((old - new) * factor) + part
                return carry

            lax.fori_loop(0, slab // small, step, 0)

        rescale_free()

        @pl.when(jnp.logical_not(jnp.max(a_ref[...]) < 1.0e38))
        def _():
            rescaled()

        m = m_ref[...]
        top = jnp.max(m, axis=0, keepdims=True)
        total = jnp.sum(a_ref[...] * jnp.exp2((m - top) * factor), axis=0, keepdims=True)
        lse = top * scaling + jnp.log(total)
        for i in range(n_blk):
            out_ref[i] = lse

    return pl.pallas_call(
        kernel,
        out_shape=(
            jax.ShapeDtypeStruct((n_blk, 1, rows), jnp.float32),
            jax.ShapeDtypeStruct((3, slots), jnp.int32),
        ),
        in_specs=vmem(2),
        out_specs=tuple(vmem(2)),
        scratch_shapes=[
            pltpu.VMEM((rows, width), jnp.bfloat16),
            pltpu.VMEM((8, rows), jnp.float32),
            pltpu.VMEM((8, rows), jnp.float32),
        ],
        compiler_params=params(16),
        name="row_pass",
    )(x, centroids)


def column_pass(x, centroids, parts, tok, scaling, all_cols, chunks):
    n_blk = x.shape[0]
    rows = n_blk * tok
    slab, width = centroids.shape
    block = slab // chunks
    group = math.gcd(chunks, 8)
    factor = scaling * log2e

    def kernel(x_ref, c_ref, l_ref, own_ref, mass_ref, t_ref, d_ref):
        load_rows(x_ref, t_ref, n_blk, tok)
        lse = l_ref[:, 0, :]
        top = jnp.max(lse, axis=0, keepdims=True)
        total = jnp.sum(jnp.exp(lse - top), axis=0, keepdims=True)
        dual = math.log(all_cols) - (top + jnp.log(total))
        position = lax.axis_index("blk")
        own = jnp.zeros((1, tok), jnp.float32)
        for i in range(n_blk):
            own = own + jnp.where(position == i, dual[:, i * tok : (i + 1) * tok], 0.0)
        own_ref[...] = own
        d_ref[...] = jnp.transpose(jnp.broadcast_to(dual * log2e, (128, rows)))

        def step(j, carry):
            for g in range(group):
                k = j * group + g
                s = lax.dot_general(
                    t_ref[...],
                    c_ref[pl.ds(pl.multiple_of(k * block, block), block), :],
                    (((1,), (1,)), ((), ())),
                    preferred_element_type=jnp.float32,
                )
                d = d_ref[...]
                e = jnp.exp2(s * factor + jnp.concatenate([d] * (block // 128), axis=1))
                mass_ref[k] = jnp.sum(e, axis=0, keepdims=True)
            return carry

        lax.fori_loop(0, chunks // group, step, 0)

    return pl.pallas_call(
        kernel,
        out_shape=(
            jax.ShapeDtypeStruct((1, tok), jnp.float32),
            jax.ShapeDtypeStruct((chunks, 1, block), jnp.float32),
        ),
        in_specs=vmem(3),
        out_specs=tuple(vmem(2)),
        scratch_shapes=[
            pltpu.VMEM((rows, width), jnp.bfloat16),
            pltpu.VMEM((rows, 128), jnp.float32),
        ],
        compiler_params=params(16),
        name="column_pass",
    )(x, centroids, parts)


def sum_and_copy(parts):
    def kernel(p_ref, out_ref):
        total = jnp.sum(p_ref[:, 0, :], axis=0, keepdims=True)
        for j in range(parts.shape[0]):
            out_ref[j] = total

    return pl.pallas_call(
        kernel,
        out_shape=jax.ShapeDtypeStruct(parts.shape, jnp.float32),
        in_specs=vmem(1),
        out_specs=pl.BlockSpec(memory_space=pltpu.VMEM),
        compiler_params=params(4),
        name="sum_and_copy",
    )(parts)


def look_up(masses, ids, all_rows, n_blk, capacity):
    chunks, _, block = masses.shape
    lines = chunks * block // 128
    slots = n_blk * capacity

    def kernel(m_ref, i_ref, dual_ref, out_ref):
        for j in range(chunks):
            for g in range(block // 128):
                k = j * (block // 128) + g
                dual_ref[k : k + 1, :] = m_ref[j, :, g * 128 : (g + 1) * 128]
        dual = math.log(all_rows) - jnp.log(dual_ref[...])
        dual_ref[...] = dual
        line = lax.broadcasted_iota(jnp.int32, (lines, slots), 0)
        pick = jnp.where(line == i_ref[0:1, :], 1.0, 0.0).astype(jnp.bfloat16)
        rest = jnp.clip(dual, -3.0e38, 3.0e38)
        found = jnp.zeros((128, slots), jnp.float32)
        for _ in range(3):
            piece = rest.astype(jnp.bfloat16)
            rest = rest - piece.astype(jnp.float32)
            found = found + lax.dot_general(
                piece, pick, (((0,), (0,)), ((), ())), preferred_element_type=jnp.float32
            )
        lane = lax.broadcasted_iota(jnp.int32, (128, slots), 0)
        value = jnp.sum(jnp.where(lane == i_ref[1:2, :], found, 0.0), axis=0, keepdims=True)
        out_ref[...] = jnp.zeros_like(out_ref)
        for i in range(n_blk):
            out_ref[i, :, :capacity] = value[:, i * capacity : (i + 1) * capacity]

    return pl.pallas_call(
        kernel,
        out_shape=(
            jax.ShapeDtypeStruct((lines, 128), jnp.float32),
            jax.ShapeDtypeStruct((n_blk, 1, 128), jnp.float32),
        ),
        in_specs=vmem(2),
        out_specs=tuple(vmem(2)),
        compiler_params=params(4),
        name="look_up",
    )(masses, ids)


def prepare(tokens, centres, row_ids, counts, duals, scaling):
    n_blk, capacity = row_ids.shape
    slots = n_blk * capacity
    tok, width = tokens.shape

    def kernel(n_ref, t_ref, c_ref, r_ref, d_ref, diff_ref, exp_ref, w_ref):
        w_ref[...] = jnp.zeros_like(w_ref)
        w_ref[:, :capacity] = r_ref[...].astype(jnp.float32)
        turned = jnp.transpose(w_ref[...])
        row = lax.broadcasted_iota(jnp.int32, (capacity, tok), 1).astype(jnp.float32)
        place = lax.broadcasted_iota(jnp.int32, (capacity, 1), 0)
        rows = t_ref[...]
        for i in range(n_blk):
            part = slice(i * capacity, (i + 1) * capacity)
            hit = row == turned[:capacity, i : i + 1]
            picked = jnp.dot(
                jnp.where(hit, 1.0, 0.0).astype(jnp.bfloat16), rows, preferred_element_type=jnp.float32
            )
            centre = c_ref[i].astype(jnp.float32)
            diff_ref[part, :] = picked - centre
            score = jnp.sum(picked * centre, axis=1, keepdims=True) * scaling
            dual = jnp.sum(jnp.where(hit, d_ref[...], 0.0), axis=1, keepdims=True)
            exponent = jnp.where(place < n_ref[0, i], score + dual, dead)
            exp_ref[part, :] = jnp.broadcast_to(exponent, (capacity, width))

    shape = jax.ShapeDtypeStruct((slots, width), jnp.float32)
    return pl.pallas_call(
        kernel,
        out_shape=(shape, shape),
        in_specs=[pl.BlockSpec(memory_space=pltpu.SMEM)] + vmem(4),
        out_specs=tuple(vmem(2)),
        scratch_shapes=[pltpu.VMEM((n_blk, 128), jnp.float32)],
        compiler_params=params(4),
        name="prepare",
    )(counts, tokens, centres, row_ids, duals)


def finish(duals, diff, exponents, n_blk, capacity):
    width = diff.shape[1]

    def kernel(g_ref, d_ref, e_ref, out_ref):
        turned = jnp.transpose(g_ref[:, 0, :])
        for i in range(n_blk):
            part = slice(i * capacity, (i + 1) * capacity)
            dual = jnp.broadcast_to(turned[:capacity, i : i + 1], (capacity, width))
            e = e_ref[part, :]
            weight = jnp.where(e > 0.1 * dead, jnp.exp(e + dual), 0.0)
            out_ref[0, i] = weight * d_ref[part, :]

    return pl.pallas_call(
        kernel,
        out_shape=jax.ShapeDtypeStruct((1, n_blk, capacity, width), jnp.float32),
        in_specs=vmem(3),
        out_specs=pl.BlockSpec(memory_space=pltpu.VMEM),
        compiler_params=params(4),
        name="finish",
    )(duals, diff, exponents)


def local(tokens, centroids, row_ids, alt_ids, counts):
    tok, width = tokens.shape
    slab = centroids.shape[0]
    n_blk = lax.axis_size("blk")
    n_wide = lax.axis_size("wide")
    scaling = score_gain / math.sqrt(width)
    capacity = alt_ids.shape[2]
    slots = n_blk * capacity

    gathered = exchange(pack(tokens, alt_ids[0]), "blk")
    lse, ids = row_pass(gathered, centroids, tok, capacity, scaling)
    parts = exchange(lse, "blk")
    centres = exchange(centroids[ids[2]].reshape(n_blk, capacity, width), "blk")
    own_duals, partial_mass = column_pass(gathered, centroids, parts, tok, scaling, slab * n_blk, n_wide)
    partial_mass, centres = lax.optimization_barrier((partial_mass, centres))

    chunk = sum_and_copy(exchange(partial_mass, "wide"))
    diff, exponents = prepare(tokens, centres, row_ids[0], counts, own_duals, scaling)
    chunk, diff, exponents = lax.optimization_barrier((chunk, diff, exponents))
    masses = exchange(chunk, "wide")
    col_duals, found = look_up(masses, ids, tok * n_blk * n_wide, n_blk, capacity)
    residuals = finish(exchange(found, "blk"), diff, exponents, n_blk, capacity)
    return (own_duals.reshape(tok), col_duals.reshape(slab), residuals)


def solution(mesh):
    in_specs = (
        P(("blk", "wide"), None),
        P("blk", None),
        P(("blk", "wide"), None, None),
        P(("blk", "wide"), None, None),
        P(("blk", "wide"), None),
    )
    out_specs = (P(("blk", "wide")), P("blk"), P(("blk", "wide"), None, None, None))
    return jax.shard_map(local, mesh=mesh, in_specs=in_specs, out_specs=out_specs, check_vma=False)
```

```python
import math

import jax
import jax.numpy as jnp
from jax import lax
from jax.experimental import pallas as pl
from jax.experimental.pallas import tpu as pltpu
from jax.sharding import PartitionSpec as P

score_gain = 3.0
log2e = 1.4426950408889634
dead = -1.0e30


def vmem(n):
    return [pl.BlockSpec(memory_space=pltpu.VMEM)] * n


def load_rows(x_ref, t_ref, n_blk, tok):
    for i in range(n_blk):
        t_ref[i * tok : (i + 1) * tok, :] = x_ref[i, :tok, :]


def exchange(x, axis, groups=None):
    return lax.all_to_all(x, axis, split_axis=0, concat_axis=0, axis_index_groups=groups, tiled=True)


def params(mib):
    return pltpu.CompilerParams(vmem_limit_bytes=mib << 20)


def stage(x):
    def kernel(x_ref, out_ref, sem):
        copy = pltpu.make_async_copy(x_ref, out_ref, sem)
        copy.start()
        copy.wait()

    return pl.pallas_call(
        kernel,
        out_shape=jax.ShapeDtypeStruct(x.shape, x.dtype),
        in_specs=[pl.BlockSpec(memory_space=pl.ANY)],
        out_specs=pl.BlockSpec(memory_space=pltpu.VMEM),
        scratch_shapes=[pltpu.SemaphoreType.DMA],
        compiler_params=params(4),
        cost_estimate=pl.CostEstimate(flops=0, transcendentals=0, bytes_accessed=2 * x.size * x.dtype.itemsize),
        name="stage",
    )(x)


def row_pass(x, centroids, alt_ids, tok, scaling):
    n_blk = x.shape[0]
    rows = n_blk * tok
    capacity = alt_ids.shape[1]
    slab, width = centroids.shape
    factor = scaling * log2e
    block = math.gcd(slab, 2048)
    small = math.gcd(slab, 256)

    def kernel(x_ref, c_ref, i_ref, out_ref, t_ref, m_ref, a_ref):
        load_rows(x_ref, t_ref, n_blk, tok)

        def scores(start, size, lanes):
            return lax.dot_general(
                c_ref[pl.ds(start, size), :],
                t_ref[lanes, :],
                (((1,), (1,)), ((), ())),
                preferred_element_type=jnp.float32,
            ).reshape(size // 8, 8, 256)

        def rescale_free():
            for g in range(rows // 256):
                lanes = slice(g * 256, (g + 1) * 256)
                first = jnp.max(scores(0, small, lanes), axis=(0, 1)).reshape(1, 256)
                m_ref[:, lanes] = jnp.broadcast_to(first, (8, 256))
            a_ref[...] = jnp.zeros_like(a_ref)

            def step(j, carry):
                start = pl.multiple_of(j * block, block)
                for g in range(rows // 256):
                    lanes = slice(g * 256, (g + 1) * 256)
                    e = jnp.exp2((scores(start, block, lanes) - m_ref[:, lanes][None]) * factor)
                    a_ref[:, lanes] = a_ref[:, lanes] + jnp.sum(e, axis=0)
                return carry

            lax.fori_loop(0, slab // block, step, 0)

        def rescaled():
            m_ref[...] = jnp.full_like(m_ref, dead)
            a_ref[...] = jnp.zeros_like(a_ref)

            def step(j, carry):
                start = pl.multiple_of(j * small, small)
                for g in range(rows // 256):
                    lanes = slice(g * 256, (g + 1) * 256)
                    s = scores(start, small, lanes)
                    old = m_ref[:, lanes]
                    new = jnp.maximum(old, jnp.max(s, axis=0))
                    m_ref[:, lanes] = new
                    part = jnp.sum(jnp.exp2((s - new[None]) * factor), axis=0)
                    a_ref[:, lanes] = a_ref[:, lanes] * jnp.exp2((old - new) * factor) + part
                return carry

            lax.fori_loop(0, slab // small, step, 0)

        rescale_free()

        @pl.when(jnp.logical_not(jnp.max(a_ref[...]) < 1.0e38))
        def _():
            rescaled()

        m = m_ref[...]
        top = jnp.max(m, axis=0, keepdims=True)
        total = jnp.sum(a_ref[...] * jnp.exp2((m - top) * factor), axis=0, keepdims=True)
        lse = top * scaling + jnp.log(total)
        ids = i_ref[...]
        line = jnp.concatenate(
            [ids >> 7, ids & 127, jnp.zeros((n_blk, 128 - 2 * capacity), jnp.int32)], axis=1
        ).astype(jnp.float32)
        for i in range(n_blk):
            out_ref[i, :, :rows] = lse
            out_ref[i, :, rows:] = line[i : i + 1, :]

    return pl.pallas_call(
        kernel,
        out_shape=jax.ShapeDtypeStruct((n_blk, 1, rows + 128), jnp.float32),
        in_specs=vmem(3),
        out_specs=pl.BlockSpec(memory_space=pltpu.VMEM),
        scratch_shapes=[
            pltpu.VMEM((rows, width), jnp.bfloat16),
            pltpu.VMEM((8, rows), jnp.float32),
            pltpu.VMEM((8, rows), jnp.float32),
        ],
        compiler_params=params(16),
        name="row_pass",
    )(x, centroids, alt_ids)


def unpack(parts, rows, capacity):
    n_blk = parts.shape[0]

    def kernel(p_ref, ids_ref):
        for i in range(n_blk):
            line = p_ref[i, :, rows:].astype(jnp.int32)
            part = slice(i * capacity, (i + 1) * capacity)
            ids_ref[0:1, part] = line[:, :capacity]
            ids_ref[1:2, part] = line[:, capacity : 2 * capacity]
            ids_ref[2:3, part] = line[:, :capacity] * 128 + line[:, capacity : 2 * capacity]

    return pl.pallas_call(
        kernel,
        out_shape=jax.ShapeDtypeStruct((3, n_blk * capacity), jnp.int32),
        in_specs=vmem(1),
        out_specs=pl.BlockSpec(memory_space=pltpu.VMEM),
        compiler_params=params(4),
        name="unpack",
    )(parts)


def column_pass(x, centroids, parts, tok, scaling, all_cols):
    n_blk = x.shape[0]
    rows = n_blk * tok
    slab, width = centroids.shape
    block = 256
    group = math.gcd(slab // block, 8)
    factor = scaling * log2e

    def kernel(x_ref, c_ref, l_ref, own_ref, mass_ref, t_ref, d_ref):
        load_rows(x_ref, t_ref, n_blk, tok)
        lse = l_ref[:, 0, :rows]
        top = jnp.max(lse, axis=0, keepdims=True)
        total = jnp.sum(jnp.exp(lse - top), axis=0, keepdims=True)
        dual = math.log(all_cols) - (top + jnp.log(total))
        position = lax.axis_index("blk")
        own = jnp.zeros((1, tok), jnp.float32)
        for i in range(n_blk):
            own = own + jnp.where(position == i, dual[:, i * tok : (i + 1) * tok], 0.0)
        own_ref[...] = own
        d_ref[...] = jnp.transpose(jnp.broadcast_to(dual * log2e, (128, rows)))

        def step(j, carry):
            for g in range(group):
                k = j * group + g
                s = lax.dot_general(
                    t_ref[...],
                    c_ref[pl.ds(pl.multiple_of(k * block, block), block), :],
                    (((1,), (1,)), ((), ())),
                    preferred_element_type=jnp.float32,
                )
                d = d_ref[...]
                e = jnp.exp2(s * factor + jnp.concatenate([d] * (block // 128), axis=1))
                mass = jnp.sum(e, axis=0, keepdims=True)
                for h in range(block // 128):
                    mass_ref[pl.ds(k * (block // 128) + h, 1), :] = mass[:, h * 128 : (h + 1) * 128]
            return carry

        lax.fori_loop(0, slab // (block * group), step, 0)

    return pl.pallas_call(
        kernel,
        out_shape=(
            jax.ShapeDtypeStruct((1, tok), jnp.float32),
            jax.ShapeDtypeStruct((slab // 128, 128), jnp.float32),
        ),
        in_specs=vmem(3),
        out_specs=tuple(vmem(2)),
        scratch_shapes=[
            pltpu.VMEM((rows, width), jnp.bfloat16),
            pltpu.VMEM((rows, 128), jnp.float32),
        ],
        compiler_params=params(16),
        name="column_pass",
    )(x, centroids, parts)


def spread(pair_mass, copies):
    half = pair_mass.shape[0] // 2

    def kernel(p_ref, out_ref):
        core = lax.rem(lax.axis_index("wide"), 2)
        part = p_ref[pl.ds(pl.multiple_of(core * half, half), half), :]
        for j in range(copies):
            out_ref[j] = part

    return pl.pallas_call(
        kernel,
        out_shape=jax.ShapeDtypeStruct((copies, half, 128), jnp.float32),
        in_specs=vmem(1),
        out_specs=pl.BlockSpec(memory_space=pltpu.VMEM),
        compiler_params=params(4),
        name="spread",
    )(pair_mass)


def add_up(parts):
    def kernel(p_ref, out_ref):
        out_ref[...] = jnp.sum(p_ref[...], axis=0)

    return pl.pallas_call(
        kernel,
        out_shape=jax.ShapeDtypeStruct(parts.shape[1:], jnp.float32),
        in_specs=vmem(1),
        out_specs=pl.BlockSpec(memory_space=pltpu.VMEM),
        compiler_params=params(4),
        name="add_up",
    )(parts)


def pieces_of(value):
    rest, pieces = jnp.clip(value, -3.0e38, 3.0e38), []
    for _ in range(3):
        piece = rest.astype(jnp.bfloat16)
        pieces.append(piece)
        rest = rest - piece.astype(jnp.float32)
    return pieces


def look_up(masses, ids, centres, all_rows, n_blk, capacity):
    lines = masses.shape[0]
    slots = n_blk * capacity

    def kernel(m_ref, i_ref, c_ref, dual_ref, out_ref):
        dual = math.log(all_rows) - jnp.log(m_ref[...])
        dual_ref[...] = dual
        line = lax.broadcasted_iota(jnp.int32, (lines, slots), 0)
        pick = jnp.where(line == i_ref[0:1, :], 1.0, 0.0).astype(jnp.bfloat16)
        lane = lax.broadcasted_iota(jnp.int32, (128, slots), 0)
        here = lane == i_ref[1:2, :]
        found = []
        for piece in pieces_of(dual):
            column = lax.dot_general(
                piece, pick, (((0,), (0,)), ((), ())), preferred_element_type=jnp.float32
            )
            found.append(jnp.sum(jnp.where(here, column, 0.0), axis=0, keepdims=True))
        blank = jnp.zeros((1, 128 - 3 * capacity), jnp.float32)
        for i in range(n_blk):
            part = slice(i * capacity, (i + 1) * capacity)
            out_ref[i, :capacity, :] = c_ref[part, :]
            row = jnp.concatenate([f[:, part] for f in found] + [blank], axis=1)
            out_ref[i, capacity:, :] = row.astype(jnp.bfloat16)

    return pl.pallas_call(
        kernel,
        out_shape=(
            jax.ShapeDtypeStruct((lines, 128), jnp.float32),
            jax.ShapeDtypeStruct((n_blk, capacity + 1, 128), jnp.bfloat16),
        ),
        in_specs=vmem(3),
        out_specs=tuple(vmem(2)),
        compiler_params=params(4),
        name="look_up",
    )(masses, ids, centres)


def prepare(tokens, row_ids, counts, duals):
    n_blk, capacity = row_ids.shape
    slots = n_blk * capacity
    tok, width = tokens.shape

    def kernel(n_ref, t_ref, r_ref, d_ref, row_ref, dual_ref, w_ref):
        w_ref[...] = jnp.zeros_like(w_ref)
        w_ref[:, :capacity] = r_ref[...].astype(jnp.float32)
        turned = jnp.transpose(w_ref[...])
        row = lax.broadcasted_iota(jnp.int32, (capacity, tok), 1).astype(jnp.float32)
        place = lax.broadcasted_iota(jnp.int32, (capacity, 1), 0)
        rows = t_ref[...]
        for i in range(n_blk):
            part = slice(i * capacity, (i + 1) * capacity)
            hit = row == turned[:capacity, i : i + 1]
            row_ref[part, :] = jnp.dot(
                jnp.where(hit, 1.0, 0.0).astype(jnp.bfloat16), rows, preferred_element_type=jnp.float32
            )
            dual = jnp.sum(jnp.where(hit, d_ref[...], 0.0), axis=1, keepdims=True)
            dual = jnp.where(place < n_ref[0, i], dual, dead)
            dual_ref[part, :] = jnp.broadcast_to(dual, (capacity, width))

    shape = jax.ShapeDtypeStruct((slots, width), jnp.float32)
    return pl.pallas_call(
        kernel,
        out_shape=(shape, shape),
        in_specs=[pl.BlockSpec(memory_space=pltpu.SMEM)] + vmem(3),
        out_specs=tuple(vmem(2)),
        scratch_shapes=[pltpu.VMEM((n_blk, 128), jnp.float32)],
        compiler_params=params(4),
        name="prepare",
    )(counts, tokens, row_ids, duals)


def finish(answers, rows, row_duals, scaling):
    n_blk, _, width = answers.shape
    capacity = rows.shape[0] // n_blk

    def kernel(g_ref, t_ref, d_ref, out_ref, w_ref):
        for i in range(n_blk):
            w_ref[i : i + 1, :] = g_ref[i, capacity:, :].astype(jnp.float32)
        pieces = w_ref[...]
        col_duals = pieces[:, :capacity]
        for k in range(1, 3):
            col_duals = col_duals + pieces[:, k * capacity : (k + 1) * capacity]
        w_ref[:, :capacity] = col_duals
        turned = jnp.transpose(w_ref[...])
        for i in range(n_blk):
            part = slice(i * capacity, (i + 1) * capacity)
            row = t_ref[part, :]
            centre = g_ref[i, :capacity, :].astype(jnp.float32)
            score = jnp.sum(row * centre, axis=1, keepdims=True) * scaling
            dual = d_ref[part, :]
            weight = jnp.where(dual > 0.1 * dead, jnp.exp(dual + (score + turned[:capacity, i : i + 1])), 0.0)
            out_ref[0, i] = weight * (row - centre)

    return pl.pallas_call(
        kernel,
        out_shape=jax.ShapeDtypeStruct((1, n_blk, capacity, width), jnp.float32),
        in_specs=vmem(3),
        out_specs=pl.BlockSpec(memory_space=pltpu.VMEM),
        scratch_shapes=[pltpu.VMEM((n_blk, 128), jnp.float32)],
        compiler_params=params(4),
        name="finish",
    )(answers, rows, row_duals)


def local(tokens, centroids, row_ids, alt_ids, counts):
    tok, width = tokens.shape
    slab = centroids.shape[0]
    n_blk = lax.axis_size("blk")
    n_wide = lax.axis_size("wide")
    scaling = score_gain / math.sqrt(width)
    capacity = alt_ids.shape[2]
    pairs = [[k, k + 1] for k in range(0, n_wide, 2)]
    same_core = [list(range(core, n_wide, 2)) for core in range(2)]

    gathered = exchange(jnp.broadcast_to(tokens[None], (n_blk, tok, width)), "blk")
    near = stage(centroids)
    parts = exchange(row_pass(gathered, near, alt_ids[0], tok, scaling), "blk")
    own_duals, mass = column_pass(gathered, near, parts, tok, scaling, slab * n_blk)
    mass = spread(lax.psum(mass, "wide", axis_index_groups=pairs), n_wide // 2)
    mass = add_up(exchange(mass, "wide", same_core))
    ids = unpack(parts, n_blk * tok, capacity)
    centres = near[ids[2]]
    rows, slot_duals = prepare(tokens, row_ids[0], counts, own_duals)
    mass, centres, rows, slot_duals = lax.optimization_barrier((mass, centres, rows, slot_duals))
    mass = lax.all_gather(mass, "wide", axis=0, axis_index_groups=pairs, tiled=True)
    col_duals, answers = look_up(mass, ids, centres, tok * n_blk * n_wide, n_blk, capacity)
    residuals = finish(exchange(answers, "blk"), rows, slot_duals, scaling)
    return (own_duals.reshape(tok), col_duals.reshape(slab), residuals)


def solution(mesh):
    in_specs = (
        P(("blk", "wide"), None),
        P("blk", None),
        P(("blk", "wide"), None, None),
        P(("blk", "wide"), None, None),
        P(("blk", "wide"), None),
    )
    out_specs = (P(("blk", "wide")), P("blk"), P(("blk", "wide"), None, None, None))
    return jax.shard_map(local, mesh=mesh, in_specs=in_specs, out_specs=out_specs, check_vma=False)
```

```python
import math

import jax
import jax.numpy as jnp
from jax import lax
from jax.experimental import pallas as pl
from jax.experimental.pallas import tpu as pltpu
from jax.sharding import PartitionSpec as P

score_gain = 3.0
log2e = 1.4426950408889634
dead = -1.0e30


def vmem(n):
    return [pl.BlockSpec(memory_space=pltpu.VMEM)] * n


def load_rows(x_ref, t_ref, n_blk, tok):
    for i in range(n_blk):
        t_ref[i * tok : (i + 1) * tok, :] = x_ref[i, :tok, :]


def exchange(x, axis, groups=None):
    return lax.all_to_all(x, axis, split_axis=0, concat_axis=0, axis_index_groups=groups, tiled=True)


def params(mib):
    return pltpu.CompilerParams(vmem_limit_bytes=mib << 20)


def stage(x):
    def kernel(x_ref, out_ref, sem):
        copy = pltpu.make_async_copy(x_ref, out_ref, sem)
        copy.start()
        copy.wait()

    return pl.pallas_call(
        kernel,
        out_shape=jax.ShapeDtypeStruct(x.shape, x.dtype),
        in_specs=[pl.BlockSpec(memory_space=pl.ANY)],
        out_specs=pl.BlockSpec(memory_space=pltpu.VMEM),
        scratch_shapes=[pltpu.SemaphoreType.DMA],
        compiler_params=params(4),
        cost_estimate=pl.CostEstimate(flops=0, transcendentals=0, bytes_accessed=2 * x.size * x.dtype.itemsize),
        name="stage",
    )(x)


def row_pass(x, centroids, alt_ids, row_ids, tok, scaling):
    n_blk = x.shape[0]
    rows = n_blk * tok
    capacity = alt_ids.shape[1]
    slab, width = centroids.shape
    factor = scaling * log2e
    block = math.gcd(slab, 8192)
    small = math.gcd(slab, 256)

    def kernel(x_ref, c_ref, i_ref, r_ref, out_ref, t_ref, m_ref, a_ref):
        load_rows(x_ref, t_ref, n_blk, tok)

        def scores(start, size, lanes):
            return lax.dot_general(
                c_ref[pl.ds(start, size), :],
                t_ref[lanes, :],
                (((1,), (1,)), ((), ())),
                preferred_element_type=jnp.float32,
            ).reshape(size // 8, 8, 256)

        def rescale_free():
            for g in range(rows // 256):
                lanes = slice(g * 256, (g + 1) * 256)
                first = jnp.max(scores(0, small, lanes), axis=(0, 1)).reshape(1, 256)
                m_ref[:, lanes] = jnp.broadcast_to(first, (8, 256))
            a_ref[...] = jnp.zeros_like(a_ref)

            def step(j, carry):
                start = pl.multiple_of(j * block, block)
                for g in range(rows // 256):
                    lanes = slice(g * 256, (g + 1) * 256)
                    e = jnp.exp2((scores(start, block, lanes) - m_ref[:, lanes][None]) * factor)
                    a_ref[:, lanes] = a_ref[:, lanes] + jnp.sum(e, axis=0)
                return carry

            lax.fori_loop(0, slab // block, step, 0)

        def rescaled():
            m_ref[...] = jnp.full_like(m_ref, dead)
            a_ref[...] = jnp.zeros_like(a_ref)

            def step(j, carry):
                start = pl.multiple_of(j * small, small)
                for g in range(rows // 256):
                    lanes = slice(g * 256, (g + 1) * 256)
                    s = scores(start, small, lanes)
                    old = m_ref[:, lanes]
                    new = jnp.maximum(old, jnp.max(s, axis=0))
                    m_ref[:, lanes] = new
                    part = jnp.sum(jnp.exp2((s - new[None]) * factor), axis=0)
                    a_ref[:, lanes] = a_ref[:, lanes] * jnp.exp2((old - new) * factor) + part
                return carry

            lax.fori_loop(0, slab // small, step, 0)

        rescale_free()

        @pl.when(jnp.logical_not(jnp.max(a_ref[...]) < 1.0e38))
        def _():
            rescaled()

        m = m_ref[...]
        top = jnp.max(m, axis=0, keepdims=True)
        total = jnp.sum(a_ref[...] * jnp.exp2((m - top) * factor), axis=0, keepdims=True)
        lse = top * scaling + jnp.log(total)
        ids = i_ref[...]
        line = jnp.concatenate(
            [ids >> 7, ids & 127, r_ref[...], jnp.zeros((n_blk, 128 - 3 * capacity), jnp.int32)], axis=1
        ).astype(jnp.float32)
        for i in range(n_blk):
            out_ref[i, :, :rows] = lse
            out_ref[i, :, rows:] = line[i : i + 1, :]

    return pl.pallas_call(
        kernel,
        out_shape=jax.ShapeDtypeStruct((n_blk, 1, rows + 128), jnp.float32),
        in_specs=vmem(4),
        out_specs=pl.BlockSpec(memory_space=pltpu.VMEM),
        scratch_shapes=[
            pltpu.VMEM((rows, width), jnp.bfloat16),
            pltpu.VMEM((8, rows), jnp.float32),
            pltpu.VMEM((8, rows), jnp.float32),
        ],
        compiler_params=params(16),
        name="row_pass",
    )(x, centroids, alt_ids, row_ids)


def unpack(parts, rows, capacity):
    n_blk = parts.shape[0]

    def kernel(p_ref, ids_ref):
        for i in range(n_blk):
            line = p_ref[i, :, rows:].astype(jnp.int32)
            part = slice(i * capacity, (i + 1) * capacity)
            ids_ref[0:1, part] = line[:, :capacity]
            ids_ref[1:2, part] = line[:, capacity : 2 * capacity]
            ids_ref[2:3, part] = line[:, :capacity] * 128 + line[:, capacity : 2 * capacity]

    return pl.pallas_call(
        kernel,
        out_shape=jax.ShapeDtypeStruct((3, n_blk * capacity), jnp.int32),
        in_specs=vmem(1),
        out_specs=pl.BlockSpec(memory_space=pltpu.VMEM),
        compiler_params=params(4),
        name="unpack",
    )(parts)


def column_pass(x, centroids, parts, tok, scaling, all_cols):
    n_blk = x.shape[0]
    rows = n_blk * tok
    slab, width = centroids.shape
    block = 256
    group = math.gcd(slab // block, 32)
    factor = scaling * log2e

    def kernel(x_ref, c_ref, l_ref, own_ref, dual_ref, mass_ref, t_ref, d_ref):
        load_rows(x_ref, t_ref, n_blk, tok)
        lse = l_ref[:, 0, :rows]
        top = jnp.max(lse, axis=0, keepdims=True)
        total = jnp.sum(jnp.exp(lse - top), axis=0, keepdims=True)
        dual = math.log(all_cols) - (top + jnp.log(total))
        dual_ref[...] = dual
        position = lax.axis_index("blk")
        own = jnp.zeros((1, tok), jnp.float32)
        for i in range(n_blk):
            own = own + jnp.where(position == i, dual[:, i * tok : (i + 1) * tok], 0.0)
        own_ref[...] = own
        d_ref[...] = jnp.transpose(jnp.broadcast_to(dual * log2e, (128, rows)))

        def step(j, carry):
            for g in range(group):
                k = j * group + g
                s = lax.dot_general(
                    t_ref[...],
                    c_ref[pl.ds(pl.multiple_of(k * block, block), block), :],
                    (((1,), (1,)), ((), ())),
                    preferred_element_type=jnp.float32,
                )
                d = d_ref[...]
                e = jnp.exp2(s * factor + jnp.concatenate([d] * (block // 128), axis=1))
                mass = jnp.sum(e, axis=0, keepdims=True)
                for h in range(block // 128):
                    mass_ref[pl.ds(k * (block // 128) + h, 1), :] = mass[:, h * 128 : (h + 1) * 128]
            return carry

        lax.fori_loop(0, slab // (block * group), step, 0)

    return pl.pallas_call(
        kernel,
        out_shape=(
            jax.ShapeDtypeStruct((1, tok), jnp.float32),
            jax.ShapeDtypeStruct((1, rows), jnp.float32),
            jax.ShapeDtypeStruct((slab // 128, 128), jnp.float32),
        ),
        in_specs=vmem(3),
        out_specs=tuple(vmem(3)),
        scratch_shapes=[
            pltpu.VMEM((rows, width), jnp.bfloat16),
            pltpu.VMEM((rows, 128), jnp.float32),
        ],
        compiler_params=params(16),
        name="column_pass",
    )(x, centroids, parts)


def spread(both, copies):
    lines = both.shape[0] // 2
    half = lines // 2

    def kernel(p_ref, out_ref):
        core = lax.rem(lax.axis_index("wide"), 2)
        start = pl.multiple_of(core * half, half)
        part = p_ref[pl.ds(start, half), :] + p_ref[pl.ds(lines + start, half), :]
        for j in range(copies):
            out_ref[j] = part

    return pl.pallas_call(
        kernel,
        out_shape=jax.ShapeDtypeStruct((copies, half, 128), jnp.float32),
        in_specs=vmem(1),
        out_specs=pl.BlockSpec(memory_space=pltpu.VMEM),
        compiler_params=params(4),
        name="spread",
    )(both)


def add_up(parts):
    def kernel(p_ref, out_ref):
        out_ref[...] = jnp.sum(p_ref[...], axis=0)

    return pl.pallas_call(
        kernel,
        out_shape=jax.ShapeDtypeStruct(parts.shape[1:], jnp.float32),
        in_specs=vmem(1),
        out_specs=pl.BlockSpec(memory_space=pltpu.VMEM),
        compiler_params=params(4),
        name="add_up",
    )(parts)


def pieces_of(value):
    rest, pieces = jnp.clip(value, -3.0e38, 3.0e38), []
    for _ in range(3):
        piece = rest.astype(jnp.bfloat16)
        pieces.append(piece)
        rest = rest - piece.astype(jnp.float32)
    return pieces


def ask_scores(x, centres, parts, duals, scaling):
    n_blk, tok, width = x.shape
    rows = n_blk * tok
    capacity = centres.shape[0] // n_blk

    def kernel(x_ref, c_ref, p_ref, d_ref, out_ref, w_ref):
        for i in range(n_blk):
            w_ref[i : i + 1, :] = p_ref[i, :, rows:]
        turned = jnp.transpose(w_ref[...])[2 * capacity : 3 * capacity, :]
        row = lax.broadcasted_iota(jnp.int32, (capacity, tok), 1).astype(jnp.float32)
        lane = lax.broadcasted_iota(jnp.int32, (capacity, 128), 1)
        table = jnp.zeros((capacity, 128), jnp.float32)
        for i in range(n_blk):
            hit = row == turned[:, i : i + 1]
            picked = jnp.dot(
                jnp.where(hit, 1.0, 0.0).astype(jnp.bfloat16), x_ref[i], preferred_element_type=jnp.float32
            )
            centre = c_ref[i * capacity : (i + 1) * capacity, :].astype(jnp.float32)
            score = jnp.sum(picked * centre, axis=1, keepdims=True) * scaling
            dual = jnp.where(hit, d_ref[:, i * tok : (i + 1) * tok], 0.0)
            dual = jnp.sum(dual, axis=1, keepdims=True)
            table = jnp.where(lane == i, score + dual, table)
        table = jnp.transpose(table)
        for i in range(n_blk):
            out_ref[:, i * capacity : (i + 1) * capacity] = table[i : i + 1, :]

    return pl.pallas_call(
        kernel,
        out_shape=jax.ShapeDtypeStruct((1, n_blk * capacity), jnp.float32),
        in_specs=vmem(4),
        out_specs=pl.BlockSpec(memory_space=pltpu.VMEM),
        scratch_shapes=[pltpu.VMEM((n_blk, 128), jnp.float32)],
        compiler_params=params(4),
        name="ask_scores",
    )(x, centres, parts, duals)


def look_up(masses, ids, centres, sums, all_rows, n_blk, capacity):
    lines = masses.shape[0]
    slots = n_blk * capacity

    def kernel(m_ref, i_ref, c_ref, s_ref, dual_ref, out_ref):
        dual = math.log(all_rows) - jnp.log(m_ref[...])
        dual_ref[...] = dual
        line = lax.broadcasted_iota(jnp.int32, (lines, slots), 0)
        pick = jnp.where(line == i_ref[0:1, :], 1.0, 0.0).astype(jnp.bfloat16)
        lane = lax.broadcasted_iota(jnp.int32, (128, slots), 0)
        here = lane == i_ref[1:2, :]
        total = jnp.zeros((128, slots), jnp.float32)
        for piece in pieces_of(dual):
            total = total + lax.dot_general(
                piece, pick, (((0,), (0,)), ((), ())), preferred_element_type=jnp.float32
            )
        total = jnp.sum(jnp.where(here, total, 0.0), axis=0, keepdims=True) + s_ref[...]
        pieces = [piece.astype(jnp.float32) for piece in pieces_of(total)]
        blank = jnp.zeros((1, 128 - 3 * capacity), jnp.float32)
        for i in range(n_blk):
            part = slice(i * capacity, (i + 1) * capacity)
            out_ref[i, :capacity, :] = c_ref[part, :]
            row = jnp.concatenate([piece[:, part] for piece in pieces] + [blank], axis=1)
            out_ref[i, capacity:, :] = row.astype(jnp.bfloat16)

    return pl.pallas_call(
        kernel,
        out_shape=(
            jax.ShapeDtypeStruct((lines, 128), jnp.float32),
            jax.ShapeDtypeStruct((n_blk, capacity + 1, 128), jnp.bfloat16),
        ),
        in_specs=vmem(4),
        out_specs=tuple(vmem(2)),
        compiler_params=params(4),
        name="look_up",
    )(masses, ids, centres, sums)


def prepare(tokens, row_ids, counts):
    n_blk, capacity = row_ids.shape
    slots = n_blk * capacity
    tok, width = tokens.shape

    def kernel(n_ref, t_ref, r_ref, row_ref, live_ref, w_ref):
        w_ref[...] = jnp.zeros_like(w_ref)
        w_ref[:, :capacity] = r_ref[...].astype(jnp.float32)
        turned = jnp.transpose(w_ref[...])
        row = lax.broadcasted_iota(jnp.int32, (capacity, tok), 1).astype(jnp.float32)
        place = lax.broadcasted_iota(jnp.int32, (1, 128), 1)
        rows = t_ref[...]
        for i in range(n_blk):
            part = slice(i * capacity, (i + 1) * capacity)
            hit = row == turned[:capacity, i : i + 1]
            row_ref[part, :] = jnp.dot(
                jnp.where(hit, 1.0, 0.0).astype(jnp.bfloat16), rows, preferred_element_type=jnp.float32
            )
            live_ref[i : i + 1, :] = jnp.where(place < n_ref[0, i], 1.0, 0.0)

    return pl.pallas_call(
        kernel,
        out_shape=(
            jax.ShapeDtypeStruct((slots, width), jnp.float32),
            jax.ShapeDtypeStruct((n_blk, 128), jnp.float32),
        ),
        in_specs=[pl.BlockSpec(memory_space=pltpu.SMEM)] + vmem(2),
        out_specs=tuple(vmem(2)),
        scratch_shapes=[pltpu.VMEM((n_blk, 128), jnp.float32)],
        compiler_params=params(4),
        name="prepare",
    )(counts, tokens, row_ids)


def finish(answers, rows, live):
    n_blk, _, width = answers.shape
    capacity = rows.shape[0] // n_blk

    def kernel(g_ref, t_ref, v_ref, out_ref, w_ref):
        for i in range(n_blk):
            w_ref[i : i + 1, :] = g_ref[i, capacity:, :].astype(jnp.float32)
        pieces = w_ref[...]
        exponent = pieces[:, :capacity]
        for k in range(1, 3):
            exponent = exponent + pieces[:, k * capacity : (k + 1) * capacity]
        w_ref[:, :capacity] = jnp.where(v_ref[:, :capacity] > 0.0, jnp.exp(exponent), 0.0)
        turned = jnp.transpose(w_ref[...])
        for i in range(n_blk):
            part = slice(i * capacity, (i + 1) * capacity)
            centre = g_ref[i, :capacity, :].astype(jnp.float32)
            out_ref[0, i] = turned[:capacity, i : i + 1] * (t_ref[part, :] - centre)

    return pl.pallas_call(
        kernel,
        out_shape=jax.ShapeDtypeStruct((1, n_blk, capacity, width), jnp.float32),
        in_specs=vmem(3),
        out_specs=pl.BlockSpec(memory_space=pltpu.VMEM),
        scratch_shapes=[pltpu.VMEM((n_blk, 128), jnp.float32)],
        compiler_params=params(4),
        name="finish",
    )(answers, rows, live)


def copies(x, count):
    def kernel(x_ref, out_ref, sems):
        moves = [pltpu.make_async_copy(x_ref, out_ref.at[i], sems.at[i]) for i in range(count)]
        for move in moves:
            move.start()
        for move in moves:
            move.wait()

    return pl.pallas_call(
        kernel,
        out_shape=jax.ShapeDtypeStruct((count,) + x.shape, x.dtype),
        in_specs=[pl.BlockSpec(memory_space=pl.ANY)],
        out_specs=pl.BlockSpec(memory_space=pl.ANY),
        scratch_shapes=[pltpu.SemaphoreType.DMA((count,))],
        name="copies",
    )(x)


def local(tokens, centroids, row_ids, alt_ids, counts):
    tok, width = tokens.shape
    slab = centroids.shape[0]
    n_blk = lax.axis_size("blk")
    n_wide = lax.axis_size("wide")
    scaling = score_gain / math.sqrt(width)
    capacity = alt_ids.shape[2]
    pairs = [[k, k + 1] for k in range(0, n_wide, 2)]
    same_core = [list(range(core, n_wide, 2)) for core in range(2)]

    gathered = exchange(copies(tokens, n_blk), "blk")
    near = stage(centroids)
    parts = exchange(row_pass(gathered, near, alt_ids[0], row_ids[0], tok, scaling), "blk")
    own_duals, duals, mass = column_pass(gathered, near, parts, tok, scaling, slab * n_blk)
    both = lax.all_gather(mass, "wide", axis=0, axis_index_groups=pairs, tiled=True)
    mass = add_up(exchange(spread(both, n_wide // 2), "wide", same_core))
    ids = unpack(parts, n_blk * tok, capacity)
    centres = near[ids[2]]
    sums = ask_scores(gathered, centres, parts, duals, scaling)
    rows, live = prepare(tokens, row_ids[0], counts)
    mass, sums, rows, live = lax.optimization_barrier((mass, sums, rows, live))
    mass = lax.all_gather(mass, "wide", axis=0, axis_index_groups=pairs, tiled=True)
    col_duals, answers = look_up(mass, ids, centres, sums, tok * n_blk * n_wide, n_blk, capacity)
    residuals = finish(exchange(answers, "blk"), rows, live)
    return (own_duals.reshape(tok), col_duals.reshape(slab), residuals)


def solution(mesh):
    in_specs = (
        P(("blk", "wide"), None),
        P("blk", None),
        P(("blk", "wide"), None, None),
        P(("blk", "wide"), None, None),
        P(("blk", "wide"), None),
    )
    out_specs = (P(("blk", "wide")), P("blk"), P(("blk", "wide"), None, None, None))
    return jax.shard_map(local, mesh=mesh, in_specs=in_specs, out_specs=out_specs, check_vma=False)
```

```python
import math

import jax
import jax.numpy as jnp
from jax import lax
from jax.experimental import pallas as pl
from jax.experimental.pallas import tpu as pltpu
from jax.sharding import PartitionSpec as P

score_gain = 3.0
log2e = 1.4426950408889634
dead = -1.0e30


def vmem(n):
    return [pl.BlockSpec(memory_space=pltpu.VMEM)] * n


def load_rows(x_ref, t_ref, n_blk, tok):
    for i in range(n_blk):
        t_ref[i * tok : (i + 1) * tok, :] = x_ref[i, :tok, :]


def exchange(x, axis, groups=None):
    return lax.all_to_all(x, axis, split_axis=0, concat_axis=0, axis_index_groups=groups, tiled=True)


def params(mib):
    return pltpu.CompilerParams(vmem_limit_bytes=mib << 20)


def stage(tokens, centroids, count):
    tok, width = tokens.shape

    def kernel(t_ref, c_ref, copies_ref, near_ref, t_scr, sems):
        first = pltpu.make_async_copy(t_ref, t_scr, sems.at[0])
        second = pltpu.make_async_copy(c_ref, near_ref, sems.at[1])
        first.start()
        second.start()
        first.wait()
        rows = t_scr[...]
        for i in range(count):
            copies_ref[i] = rows
        second.wait()

    return pl.pallas_call(
        kernel,
        out_shape=(
            pltpu.VMEM((count, tok, width), tokens.dtype),
            pltpu.VMEM(centroids.shape, centroids.dtype),
        ),
        in_specs=[pl.BlockSpec(memory_space=pltpu.HBM)] * 2,
        out_specs=tuple(vmem(2)),
        scratch_shapes=[pltpu.VMEM((tok, width), tokens.dtype), pltpu.SemaphoreType.DMA((2,))],
        compiler_params=params(56),
        name="stage",
    )(tokens, centroids)


def row_pass(x, centroids, alt_ids, row_ids, tok, scaling):
    n_blk = x.shape[0]
    rows = n_blk * tok
    capacity = alt_ids.shape[1]
    slab, width = centroids.shape
    factor = scaling * log2e
    block = math.gcd(slab, 8192)
    small = math.gcd(slab, 256)

    def kernel(x_ref, c_ref, i_ref, r_ref, out_ref, t_ref, m_ref, a_ref):
        load_rows(x_ref, t_ref, n_blk, tok)

        def scores(start, size, lanes):
            return lax.dot_general(
                c_ref[pl.ds(start, size), :],
                t_ref[lanes, :],
                (((1,), (1,)), ((), ())),
                preferred_element_type=jnp.float32,
            ).reshape(size // 8, 8, 256)

        def rescale_free():
            for g in range(rows // 256):
                lanes = slice(g * 256, (g + 1) * 256)
                first = jnp.max(scores(0, small, lanes), axis=(0, 1)).reshape(1, 256)
                m_ref[:, lanes] = jnp.broadcast_to(first, (8, 256))
            a_ref[...] = jnp.zeros_like(a_ref)

            def step(j, carry):
                start = pl.multiple_of(j * block, block)
                for g in range(rows // 256):
                    lanes = slice(g * 256, (g + 1) * 256)
                    e = jnp.exp2((scores(start, block, lanes) - m_ref[:, lanes][None]) * factor)
                    a_ref[:, lanes] = a_ref[:, lanes] + jnp.sum(e, axis=0)
                return carry

            lax.fori_loop(0, slab // block, step, 0)

        def rescaled():
            m_ref[...] = jnp.full_like(m_ref, dead)
            a_ref[...] = jnp.zeros_like(a_ref)

            def step(j, carry):
                start = pl.multiple_of(j * small, small)
                for g in range(rows // 256):
                    lanes = slice(g * 256, (g + 1) * 256)
                    s = scores(start, small, lanes)
                    old = m_ref[:, lanes]
                    new = jnp.maximum(old, jnp.max(s, axis=0))
                    m_ref[:, lanes] = new
                    part = jnp.sum(jnp.exp2((s - new[None]) * factor), axis=0)
                    a_ref[:, lanes] = a_ref[:, lanes] * jnp.exp2((old - new) * factor) + part
                return carry

            lax.fori_loop(0, slab // small, step, 0)

        rescale_free()

        @pl.when(jnp.logical_not(jnp.max(a_ref[...]) < 1.0e38))
        def _():
            rescaled()

        m = m_ref[...]
        top = jnp.max(m, axis=0, keepdims=True)
        total = jnp.sum(a_ref[...] * jnp.exp2((m - top) * factor), axis=0, keepdims=True)
        lse = top * scaling + jnp.log(total)
        ids = i_ref[...]
        line = jnp.concatenate(
            [ids >> 7, ids & 127, r_ref[...], jnp.zeros((n_blk, 128 - 3 * capacity), jnp.int32)], axis=1
        ).astype(jnp.float32)
        for i in range(n_blk):
            out_ref[i, :, :rows] = lse
            out_ref[i, :, rows:] = line[i : i + 1, :]

    return pl.pallas_call(
        kernel,
        out_shape=jax.ShapeDtypeStruct((n_blk, 1, rows + 128), jnp.float32),
        in_specs=vmem(4),
        out_specs=pl.BlockSpec(memory_space=pltpu.VMEM),
        scratch_shapes=[
            pltpu.VMEM((rows, width), jnp.bfloat16),
            pltpu.VMEM((8, rows), jnp.float32),
            pltpu.VMEM((8, rows), jnp.float32),
        ],
        compiler_params=params(16),
        name="row_pass",
    )(x, centroids, alt_ids, row_ids)


def unpack(parts, rows, capacity):
    n_blk = parts.shape[0]

    def kernel(p_ref, ids_ref):
        for i in range(n_blk):
            line = p_ref[i, :, rows:].astype(jnp.int32)
            part = slice(i * capacity, (i + 1) * capacity)
            ids_ref[0:1, part] = line[:, :capacity]
            ids_ref[1:2, part] = line[:, capacity : 2 * capacity]
            ids_ref[2:3, part] = line[:, :capacity] * 128 + line[:, capacity : 2 * capacity]

    return pl.pallas_call(
        kernel,
        out_shape=jax.ShapeDtypeStruct((3, n_blk * capacity), jnp.int32),
        in_specs=vmem(1),
        out_specs=pl.BlockSpec(memory_space=pltpu.VMEM),
        compiler_params=params(4),
        name="unpack",
    )(parts)


def column_pass(x, centroids, parts, tok, scaling, all_cols):
    n_blk = x.shape[0]
    rows = n_blk * tok
    slab, width = centroids.shape
    block = 256
    group = math.gcd(slab // block, 32)
    factor = scaling * log2e

    def kernel(x_ref, c_ref, l_ref, own_ref, dual_ref, mass_ref, t_ref, d_ref):
        load_rows(x_ref, t_ref, n_blk, tok)
        lse = l_ref[:, 0, :rows]
        top = jnp.max(lse, axis=0, keepdims=True)
        total = jnp.sum(jnp.exp(lse - top), axis=0, keepdims=True)
        dual = math.log(all_cols) - (top + jnp.log(total))
        dual_ref[...] = dual
        position = lax.axis_index("blk")
        own = jnp.zeros((1, tok), jnp.float32)
        for i in range(n_blk):
            own = own + jnp.where(position == i, dual[:, i * tok : (i + 1) * tok], 0.0)
        own_ref[...] = own
        d_ref[...] = jnp.transpose(jnp.broadcast_to(dual * log2e, (128, rows)))

        def step(j, carry):
            for g in range(group):
                k = j * group + g
                s = lax.dot_general(
                    t_ref[...],
                    c_ref[pl.ds(pl.multiple_of(k * block, block), block), :],
                    (((1,), (1,)), ((), ())),
                    preferred_element_type=jnp.float32,
                )
                d = d_ref[...]
                e = jnp.exp2(s * factor + jnp.concatenate([d] * (block // 128), axis=1))
                mass = jnp.sum(e, axis=0, keepdims=True)
                for h in range(block // 128):
                    mass_ref[pl.ds(k * (block // 128) + h, 1), :] = mass[:, h * 128 : (h + 1) * 128]
            return carry

        lax.fori_loop(0, slab // (block * group), step, 0)

    return pl.pallas_call(
        kernel,
        out_shape=(
            jax.ShapeDtypeStruct((1, tok), jnp.float32),
            jax.ShapeDtypeStruct((1, rows), jnp.float32),
            jax.ShapeDtypeStruct((slab // 128, 128), jnp.float32),
        ),
        in_specs=vmem(3),
        out_specs=tuple(vmem(3)),
        scratch_shapes=[
            pltpu.VMEM((rows, width), jnp.bfloat16),
            pltpu.VMEM((rows, 128), jnp.float32),
        ],
        compiler_params=params(16),
        name="column_pass",
    )(x, centroids, parts)


def spread(both, copies):
    lines = both.shape[0] // 2
    half = lines // 2

    def kernel(p_ref, out_ref):
        core = lax.rem(lax.axis_index("wide"), 2)
        start = pl.multiple_of(core * half, half)
        part = p_ref[pl.ds(start, half), :] + p_ref[pl.ds(lines + start, half), :]
        for j in range(copies):
            out_ref[j] = part

    return pl.pallas_call(
        kernel,
        out_shape=jax.ShapeDtypeStruct((copies, half, 128), jnp.float32),
        in_specs=vmem(1),
        out_specs=pl.BlockSpec(memory_space=pltpu.VMEM),
        compiler_params=params(4),
        name="spread",
    )(both)


def add_up(parts):
    def kernel(p_ref, out_ref):
        out_ref[...] = jnp.sum(p_ref[...], axis=0)

    return pl.pallas_call(
        kernel,
        out_shape=jax.ShapeDtypeStruct(parts.shape[1:], jnp.float32),
        in_specs=vmem(1),
        out_specs=pl.BlockSpec(memory_space=pltpu.VMEM),
        compiler_params=params(4),
        name="add_up",
    )(parts)


def pieces_of(value):
    rest, pieces = jnp.clip(value, -3.0e38, 3.0e38), []
    for _ in range(3):
        piece = rest.astype(jnp.bfloat16)
        pieces.append(piece)
        rest = rest - piece.astype(jnp.float32)
    return pieces


def ask_scores(x, centres, parts, duals, scaling):
    n_blk, tok, width = x.shape
    rows = n_blk * tok
    capacity = centres.shape[0] // n_blk

    def kernel(x_ref, c_ref, p_ref, d_ref, out_ref, w_ref):
        for i in range(n_blk):
            w_ref[i : i + 1, :] = p_ref[i, :, rows:]
        turned = jnp.transpose(w_ref[...])[2 * capacity : 3 * capacity, :]
        row = lax.broadcasted_iota(jnp.int32, (capacity, tok), 1).astype(jnp.float32)
        lane = lax.broadcasted_iota(jnp.int32, (capacity, 128), 1)
        table = jnp.zeros((capacity, 128), jnp.float32)
        for i in range(n_blk):
            hit = row == turned[:, i : i + 1]
            picked = jnp.dot(
                jnp.where(hit, 1.0, 0.0).astype(jnp.bfloat16), x_ref[i], preferred_element_type=jnp.float32
            )
            centre = c_ref[i * capacity : (i + 1) * capacity, :].astype(jnp.float32)
            score = jnp.sum(picked * centre, axis=1, keepdims=True) * scaling
            dual = jnp.where(hit, d_ref[:, i * tok : (i + 1) * tok], 0.0)
            dual = jnp.sum(dual, axis=1, keepdims=True)
            table = jnp.where(lane == i, score + dual, table)
        table = jnp.transpose(table)
        for i in range(n_blk):
            out_ref[:, i * capacity : (i + 1) * capacity] = table[i : i + 1, :]

    return pl.pallas_call(
        kernel,
        out_shape=jax.ShapeDtypeStruct((1, n_blk * capacity), jnp.float32),
        in_specs=vmem(4),
        out_specs=pl.BlockSpec(memory_space=pltpu.VMEM),
        scratch_shapes=[pltpu.VMEM((n_blk, 128), jnp.float32)],
        compiler_params=params(4),
        name="ask_scores",
    )(x, centres, parts, duals)


def look_up(masses, ids, centres, sums, all_rows, n_blk, capacity):
    lines = masses.shape[0]
    slots = n_blk * capacity

    def kernel(m_ref, i_ref, c_ref, s_ref, dual_ref, out_ref):
        dual = math.log(all_rows) - jnp.log(m_ref[...])
        dual_ref[...] = dual
        line = lax.broadcasted_iota(jnp.int32, (lines, slots), 0)
        pick = jnp.where(line == i_ref[0:1, :], 1.0, 0.0).astype(jnp.bfloat16)
        lane = lax.broadcasted_iota(jnp.int32, (128, slots), 0)
        here = lane == i_ref[1:2, :]
        total = jnp.zeros((128, slots), jnp.float32)
        for piece in pieces_of(dual):
            total = total + lax.dot_general(
                piece, pick, (((0,), (0,)), ((), ())), preferred_element_type=jnp.float32
            )
        total = jnp.sum(jnp.where(here, total, 0.0), axis=0, keepdims=True) + s_ref[...]
        pieces = [piece.astype(jnp.float32) for piece in pieces_of(total)]
        blank = jnp.zeros((1, 128 - 3 * capacity), jnp.float32)
        for i in range(n_blk):
            part = slice(i * capacity, (i + 1) * capacity)
            out_ref[i, :capacity, :] = c_ref[part, :]
            row = jnp.concatenate([piece[:, part] for piece in pieces] + [blank], axis=1)
            out_ref[i, capacity:, :] = row.astype(jnp.bfloat16)

    return pl.pallas_call(
        kernel,
        out_shape=(
            jax.ShapeDtypeStruct((lines, 128), jnp.float32),
            jax.ShapeDtypeStruct((n_blk, capacity + 1, 128), jnp.bfloat16),
        ),
        in_specs=vmem(4),
        out_specs=tuple(vmem(2)),
        compiler_params=params(4),
        name="look_up",
    )(masses, ids, centres, sums)


def prepare(tokens, row_ids, counts):
    n_blk, capacity = row_ids.shape
    slots = n_blk * capacity
    tok, width = tokens.shape

    def kernel(n_ref, t_ref, r_ref, row_ref, live_ref, w_ref):
        w_ref[...] = jnp.zeros_like(w_ref)
        w_ref[:, :capacity] = r_ref[...].astype(jnp.float32)
        turned = jnp.transpose(w_ref[...])
        row = lax.broadcasted_iota(jnp.int32, (capacity, tok), 1).astype(jnp.float32)
        place = lax.broadcasted_iota(jnp.int32, (1, 128), 1)
        rows = t_ref[...]
        for i in range(n_blk):
            part = slice(i * capacity, (i + 1) * capacity)
            hit = row == turned[:capacity, i : i + 1]
            row_ref[part, :] = jnp.dot(
                jnp.where(hit, 1.0, 0.0).astype(jnp.bfloat16), rows, preferred_element_type=jnp.float32
            )
            live_ref[i : i + 1, :] = jnp.where(place < n_ref[0, i], 1.0, 0.0)

    return pl.pallas_call(
        kernel,
        out_shape=(
            jax.ShapeDtypeStruct((slots, width), jnp.float32),
            jax.ShapeDtypeStruct((n_blk, 128), jnp.float32),
        ),
        in_specs=[pl.BlockSpec(memory_space=pltpu.SMEM)] + vmem(2),
        out_specs=tuple(vmem(2)),
        scratch_shapes=[pltpu.VMEM((n_blk, 128), jnp.float32)],
        compiler_params=params(4),
        name="prepare",
    )(counts, tokens, row_ids)


def finish(answers, rows, live):
    n_blk, _, width = answers.shape
    capacity = rows.shape[0] // n_blk

    def kernel(g_ref, t_ref, v_ref, out_ref, w_ref):
        for i in range(n_blk):
            w_ref[i : i + 1, :] = g_ref[i, capacity:, :].astype(jnp.float32)
        pieces = w_ref[...]
        exponent = pieces[:, :capacity]
        for k in range(1, 3):
            exponent = exponent + pieces[:, k * capacity : (k + 1) * capacity]
        w_ref[:, :capacity] = jnp.where(v_ref[:, :capacity] > 0.0, jnp.exp(exponent), 0.0)
        turned = jnp.transpose(w_ref[...])
        for i in range(n_blk):
            part = slice(i * capacity, (i + 1) * capacity)
            centre = g_ref[i, :capacity, :].astype(jnp.float32)
            out_ref[0, i] = turned[:capacity, i : i + 1] * (t_ref[part, :] - centre)

    return pl.pallas_call(
        kernel,
        out_shape=jax.ShapeDtypeStruct((1, n_blk, capacity, width), jnp.float32),
        in_specs=vmem(3),
        out_specs=pl.BlockSpec(memory_space=pltpu.VMEM),
        scratch_shapes=[pltpu.VMEM((n_blk, 128), jnp.float32)],
        compiler_params=params(4),
        name="finish",
    )(answers, rows, live)


def local(tokens, centroids, row_ids, alt_ids, counts):
    tok, width = tokens.shape
    slab = centroids.shape[0]
    n_blk = lax.axis_size("blk")
    n_wide = lax.axis_size("wide")
    scaling = score_gain / math.sqrt(width)
    capacity = alt_ids.shape[2]
    pairs = [[k, k + 1] for k in range(0, n_wide, 2)]
    same_core = [list(range(core, n_wide, 2)) for core in range(2)]

    outgoing, near = stage(tokens, centroids, n_blk)
    gathered = exchange(outgoing, "blk")
    parts = exchange(row_pass(gathered, near, alt_ids[0], row_ids[0], tok, scaling), "blk")
    own_duals, duals, mass = column_pass(gathered, near, parts, tok, scaling, slab * n_blk)
    both = lax.all_gather(mass, "wide", axis=0, axis_index_groups=pairs, tiled=True)
    mass = add_up(exchange(spread(both, n_wide // 2), "wide", same_core))
    ids = unpack(parts, n_blk * tok, capacity)
    centres = near[ids[2]]
    sums = ask_scores(gathered, centres, parts, duals, scaling)
    rows, live = prepare(tokens, row_ids[0], counts)
    mass, sums, rows, live = lax.optimization_barrier((mass, sums, rows, live))
    mass = lax.all_gather(mass, "wide", axis=0, axis_index_groups=pairs, tiled=True)
    col_duals, answers = look_up(mass, ids, centres, sums, tok * n_blk * n_wide, n_blk, capacity)
    residuals = finish(exchange(answers, "blk"), rows, live)
    return (own_duals.reshape(tok), col_duals.reshape(slab), residuals)


def solution(mesh):
    in_specs = (
        P(("blk", "wide"), None),
        P("blk", None),
        P(("blk", "wide"), None, None),
        P(("blk", "wide"), None, None),
        P(("blk", "wide"), None),
    )
    out_specs = (P(("blk", "wide")), P("blk"), P(("blk", "wide"), None, None, None))
    return jax.shard_map(local, mesh=mesh, in_specs=in_specs, out_specs=out_specs, check_vma=False)
```

```python
import math

import jax
import jax.numpy as jnp
from jax import lax
from jax.experimental import pallas as pl
from jax.experimental.pallas import tpu as pltpu
from jax.sharding import PartitionSpec as P

score_gain = 3.0
log2e = 1.4426950408889634
dead = -1.0e30


def vmem(n):
    return [pl.BlockSpec(memory_space=pltpu.VMEM)] * n


def load_rows(x_ref, t_ref, n_blk, tok):
    for i in range(n_blk):
        t_ref[i * tok : (i + 1) * tok, :] = x_ref[i, :tok, :]


def exchange(x, axis, groups=None):
    return lax.all_to_all(x, axis, split_axis=0, concat_axis=0, axis_index_groups=groups, tiled=True)


def params(mib):
    return pltpu.CompilerParams(vmem_limit_bytes=mib << 20)


def stage(tokens, centroids, count):
    tok, width = tokens.shape

    def kernel(t_ref, c_ref, copies_ref, near_ref, t_scr, sems):
        first = pltpu.make_async_copy(t_ref, t_scr, sems.at[0])
        second = pltpu.make_async_copy(c_ref, near_ref, sems.at[1])
        first.start()
        second.start()
        first.wait()
        rows = t_scr[...]
        for i in range(count):
            copies_ref[i] = rows
        second.wait()

    return pl.pallas_call(
        kernel,
        out_shape=(
            pltpu.VMEM((count, tok, width), tokens.dtype),
            pltpu.VMEM(centroids.shape, centroids.dtype),
        ),
        in_specs=[pl.BlockSpec(memory_space=pltpu.HBM)] * 2,
        out_specs=tuple(vmem(2)),
        scratch_shapes=[pltpu.VMEM((tok, width), tokens.dtype), pltpu.SemaphoreType.DMA((2,))],
        compiler_params=params(56),
        name="stage",
    )(tokens, centroids)


def row_pass(x, centroids, alt_ids, row_ids, tok, scaling):
    n_blk = x.shape[0]
    rows = n_blk * tok
    capacity = alt_ids.shape[1]
    slab, width = centroids.shape
    factor = scaling * log2e
    block = math.gcd(slab, 1024)
    small = math.gcd(slab, 256)
    height = 256

    def kernel(x_ref, c_ref, i_ref, r_ref, out_ref, e_ref, base_ref, t_ref, s_ref, m_ref, a_ref, l_ref):
        load_rows(x_ref, t_ref, n_blk, tok)

        def scores(band, start, size):
            return lax.dot_general(
                t_ref[band, :],
                c_ref[start : start + size, :],
                (((1,), (1,)), ((), ())),
                preferred_element_type=jnp.float32,
            )

        bands = [slice(r, r + height) for r in range(0, rows, height)]
        for band in bands:
            first = jnp.max(scores(band, 0, small), axis=1, keepdims=True)
            base_ref[band, :] = jnp.broadcast_to(first, (height, 128))
        s_ref[...] = jnp.zeros_like(s_ref)
        for start in range(0, slab, block):
            for band in bands:
                s = scores(band, start, block)
                total = s_ref[band, :]
                for g in range(0, block, 128):
                    e = jnp.exp2((s[:, g : g + 128] - base_ref[band, :]) * factor)
                    e_ref[band, start + g : start + g + 128] = e
                    total = total + e
                s_ref[band, :] = total
        base = jnp.transpose(base_ref[...])[:1, :]
        total = jnp.sum(jnp.transpose(s_ref[...]), axis=0, keepdims=True)
        l_ref[...] = base * scaling + jnp.log(total)

        @pl.when(jnp.logical_not(jnp.max(total) < 1.0e15))
        def _():
            m_ref[...] = jnp.full_like(m_ref, dead)
            a_ref[...] = jnp.zeros_like(a_ref)

            def step(j, carry):
                start = pl.multiple_of(j * small, small)
                e_ref[:, pl.ds(start, small)] = jnp.zeros((rows, small), jnp.float32)
                for g in range(0, rows, 256):
                    lanes = slice(g, g + 256)
                    s = lax.dot_general(
                        c_ref[pl.ds(start, small), :],
                        t_ref[lanes, :],
                        (((1,), (1,)), ((), ())),
                        preferred_element_type=jnp.float32,
                    ).reshape(small // 8, 8, 256)
                    old = m_ref[:, lanes]
                    new = jnp.maximum(old, jnp.max(s, axis=0))
                    m_ref[:, lanes] = new
                    part = jnp.sum(jnp.exp2((s - new[None]) * factor), axis=0)
                    a_ref[:, lanes] = a_ref[:, lanes] * jnp.exp2((old - new) * factor) + part
                return carry

            lax.fori_loop(0, slab // small, step, 0)
            m = m_ref[...]
            top = jnp.max(m, axis=0, keepdims=True)
            sums = jnp.sum(a_ref[...] * jnp.exp2((m - top) * factor), axis=0, keepdims=True)
            l_ref[...] = top * scaling + jnp.log(sums)

        lse = l_ref[...]
        ids = i_ref[...]
        line = jnp.concatenate(
            [ids >> 7, ids & 127, r_ref[...], jnp.zeros((n_blk, 128 - 3 * capacity), jnp.int32)], axis=1
        ).astype(jnp.float32)
        for i in range(n_blk):
            out_ref[i, :, :rows] = lse
            out_ref[i, :, rows:] = line[i : i + 1, :]

    return pl.pallas_call(
        kernel,
        out_shape=(
            jax.ShapeDtypeStruct((n_blk, 1, rows + 128), jnp.float32),
            pltpu.VMEM((rows, slab), jnp.float32),
            pltpu.VMEM((rows, 128), jnp.float32),
        ),
        in_specs=vmem(4),
        out_specs=tuple(vmem(3)),
        scratch_shapes=[
            pltpu.VMEM((rows, width), jnp.bfloat16),
            pltpu.VMEM((rows, 128), jnp.float32),
            pltpu.VMEM((8, rows), jnp.float32),
            pltpu.VMEM((8, rows), jnp.float32),
            pltpu.VMEM((1, rows), jnp.float32),
        ],
        compiler_params=params(8),
        name="row_pass",
    )(x, centroids, alt_ids, row_ids)


def unpack(parts, rows, capacity):
    n_blk = parts.shape[0]

    def kernel(p_ref, ids_ref):
        for i in range(n_blk):
            line = p_ref[i, :, rows:].astype(jnp.int32)
            part = slice(i * capacity, (i + 1) * capacity)
            ids_ref[0:1, part] = line[:, :capacity]
            ids_ref[1:2, part] = line[:, capacity : 2 * capacity]
            ids_ref[2:3, part] = line[:, :capacity] * 128 + line[:, capacity : 2 * capacity]

    return pl.pallas_call(
        kernel,
        out_shape=jax.ShapeDtypeStruct((3, n_blk * capacity), jnp.int32),
        in_specs=vmem(1),
        out_specs=pl.BlockSpec(memory_space=pltpu.VMEM),
        compiler_params=params(4),
        name="unpack",
    )(parts)


def column_pass(x, centroids, parts, kept, base, tok, scaling, all_cols):
    n_blk = x.shape[0]
    rows = n_blk * tok
    slab, width = centroids.shape
    block = 256
    factor = scaling * log2e
    lines = slab // 128
    held = math.gcd(lines, 32)

    def kernel(x_ref, c_ref, l_ref, e_ref, b_ref, own_ref, dual_ref, mass_ref, t_ref, d_ref, w_ref):
        lse = l_ref[:, 0, :rows]
        top = jnp.max(lse, axis=0, keepdims=True)
        total = jnp.sum(jnp.exp(lse - top), axis=0, keepdims=True)
        dual = math.log(all_cols) - (top + jnp.log(total))
        dual_ref[...] = dual
        position = lax.axis_index("blk")
        own = jnp.zeros((1, tok), jnp.float32)
        for i in range(n_blk):
            own = own + jnp.where(position == i, dual[:, i * tok : (i + 1) * tok], 0.0)
        own_ref[...] = own
        d_ref[...] = jnp.transpose(jnp.broadcast_to(dual * log2e, (128, rows)))
        w_ref[...] = jnp.exp2(b_ref[...] * factor + d_ref[...])

        for first in range(0, lines, held):

            def add(r, sums):
                sums = list(sums)
                start = pl.multiple_of(r * 32, 32)
                for q in range(0, 32, 8):
                    w = w_ref[pl.ds(start + q, 8), :]
                    for g in range(held):
                        k = (first + g) * 128
                        sums[g] = sums[g] + e_ref[pl.ds(start + q, 8), k : k + 128] * w
                return tuple(sums)

            sums = lax.fori_loop(0, rows // 32, add, tuple(jnp.zeros((8, 128), jnp.float32) for _ in range(held)))
            for g in range(held):
                mass_ref[first + g : first + g + 1, :] = jnp.sum(sums[g], axis=0, keepdims=True)

        mass = mass_ref[...]
        sound = jnp.logical_and(jnp.min(mass) > 1.0e-12, jnp.max(mass) < 1.0e12)

        @pl.when(jnp.logical_not(sound))
        def _():
            load_rows(x_ref, t_ref, n_blk, tok)

            def step(k, carry):
                s = lax.dot_general(
                    t_ref[...],
                    c_ref[pl.ds(pl.multiple_of(k * block, block), block), :],
                    (((1,), (1,)), ((), ())),
                    preferred_element_type=jnp.float32,
                )
                d = d_ref[...]
                e = jnp.exp2(s * factor + jnp.concatenate([d] * (block // 128), axis=1))
                part = jnp.sum(e, axis=0, keepdims=True)
                for h in range(block // 128):
                    mass_ref[pl.ds(k * (block // 128) + h, 1), :] = part[:, h * 128 : (h + 1) * 128]
                return carry

            lax.fori_loop(0, slab // block, step, 0)

    return pl.pallas_call(
        kernel,
        out_shape=(
            jax.ShapeDtypeStruct((1, tok), jnp.float32),
            jax.ShapeDtypeStruct((1, rows), jnp.float32),
            jax.ShapeDtypeStruct((lines, 128), jnp.float32),
        ),
        in_specs=vmem(5),
        out_specs=tuple(vmem(3)),
        scratch_shapes=[
            pltpu.VMEM((rows, width), jnp.bfloat16),
            pltpu.VMEM((rows, 128), jnp.float32),
            pltpu.VMEM((rows, 128), jnp.float32),
        ],
        compiler_params=params(8),
        name="column_pass",
    )(x, centroids, parts, kept, base)


def spread(both, copies):
    lines = both.shape[0] // 2
    half = lines // 2

    def kernel(p_ref, out_ref):
        core = lax.rem(lax.axis_index("wide"), 2)
        start = pl.multiple_of(core * half, half)
        part = p_ref[pl.ds(start, half), :] + p_ref[pl.ds(lines + start, half), :]
        for j in range(copies):
            out_ref[j] = part

    return pl.pallas_call(
        kernel,
        out_shape=jax.ShapeDtypeStruct((copies, half, 128), jnp.float32),
        in_specs=vmem(1),
        out_specs=pl.BlockSpec(memory_space=pltpu.VMEM),
        compiler_params=params(4),
        name="spread",
    )(both)


def add_up(parts):
    def kernel(p_ref, out_ref):
        out_ref[...] = jnp.sum(p_ref[...], axis=0)

    return pl.pallas_call(
        kernel,
        out_shape=jax.ShapeDtypeStruct(parts.shape[1:], jnp.float32),
        in_specs=vmem(1),
        out_specs=pl.BlockSpec(memory_space=pltpu.VMEM),
        compiler_params=params(4),
        name="add_up",
    )(parts)


def pieces_of(value):
    rest, pieces = jnp.clip(value, -3.0e38, 3.0e38), []
    for _ in range(3):
        piece = rest.astype(jnp.bfloat16)
        pieces.append(piece)
        rest = rest - piece.astype(jnp.float32)
    return pieces


def ask_scores(x, centres, parts, duals, scaling):
    n_blk, tok, width = x.shape
    rows = n_blk * tok
    capacity = centres.shape[0] // n_blk

    def kernel(x_ref, c_ref, p_ref, d_ref, out_ref, w_ref):
        for i in range(n_blk):
            w_ref[i : i + 1, :] = p_ref[i, :, rows:]
        turned = jnp.transpose(w_ref[...])[2 * capacity : 3 * capacity, :]
        row = lax.broadcasted_iota(jnp.int32, (capacity, tok), 1).astype(jnp.float32)
        lane = lax.broadcasted_iota(jnp.int32, (capacity, 128), 1)
        table = jnp.zeros((capacity, 128), jnp.float32)
        for i in range(n_blk):
            hit = row == turned[:, i : i + 1]
            picked = jnp.dot(
                jnp.where(hit, 1.0, 0.0).astype(jnp.bfloat16), x_ref[i], preferred_element_type=jnp.float32
            )
            centre = c_ref[i * capacity : (i + 1) * capacity, :].astype(jnp.float32)
            score = jnp.sum(picked * centre, axis=1, keepdims=True) * scaling
            dual = jnp.where(hit, d_ref[:, i * tok : (i + 1) * tok], 0.0)
            dual = jnp.sum(dual, axis=1, keepdims=True)
            table = jnp.where(lane == i, score + dual, table)
        table = jnp.transpose(table)
        for i in range(n_blk):
            out_ref[:, i * capacity : (i + 1) * capacity] = table[i : i + 1, :]

    return pl.pallas_call(
        kernel,
        out_shape=jax.ShapeDtypeStruct((1, n_blk * capacity), jnp.float32),
        in_specs=vmem(4),
        out_specs=pl.BlockSpec(memory_space=pltpu.VMEM),
        scratch_shapes=[pltpu.VMEM((n_blk, 128), jnp.float32)],
        compiler_params=params(4),
        name="ask_scores",
    )(x, centres, parts, duals)


def look_up(masses, ids, centres, sums, all_rows, n_blk, capacity):
    lines = masses.shape[0]
    slots = n_blk * capacity

    def kernel(m_ref, i_ref, c_ref, s_ref, dual_ref, out_ref):
        dual = math.log(all_rows) - jnp.log(m_ref[...])
        dual_ref[...] = dual
        line = lax.broadcasted_iota(jnp.int32, (lines, slots), 0)
        pick = jnp.where(line == i_ref[0:1, :], 1.0, 0.0).astype(jnp.bfloat16)
        lane = lax.broadcasted_iota(jnp.int32, (128, slots), 0)
        here = lane == i_ref[1:2, :]
        total = jnp.zeros((128, slots), jnp.float32)
        for piece in pieces_of(dual):
            total = total + lax.dot_general(
                piece, pick, (((0,), (0,)), ((), ())), preferred_element_type=jnp.float32
            )
        total = jnp.sum(jnp.where(here, total, 0.0), axis=0, keepdims=True) + s_ref[...]
        pieces = [piece.astype(jnp.float32) for piece in pieces_of(total)]
        blank = jnp.zeros((1, 128 - 3 * capacity), jnp.float32)
        for i in range(n_blk):
            part = slice(i * capacity, (i + 1) * capacity)
            out_ref[i, :capacity, :] = c_ref[part, :]
            row = jnp.concatenate([piece[:, part] for piece in pieces] + [blank], axis=1)
            out_ref[i, capacity:, :] = row.astype(jnp.bfloat16)

    return pl.pallas_call(
        kernel,
        out_shape=(
            jax.ShapeDtypeStruct((lines, 128), jnp.float32),
            jax.ShapeDtypeStruct((n_blk, capacity + 1, 128), jnp.bfloat16),
        ),
        in_specs=vmem(4),
        out_specs=tuple(vmem(2)),
        compiler_params=params(4),
        name="look_up",
    )(masses, ids, centres, sums)


def prepare(tokens, row_ids, counts):
    n_blk, capacity = row_ids.shape
    slots = n_blk * capacity
    tok, width = tokens.shape

    def kernel(n_ref, t_ref, r_ref, row_ref, live_ref, w_ref):
        w_ref[...] = jnp.zeros_like(w_ref)
        w_ref[:, :capacity] = r_ref[...].astype(jnp.float32)
        turned = jnp.transpose(w_ref[...])
        row = lax.broadcasted_iota(jnp.int32, (capacity, tok), 1).astype(jnp.float32)
        place = lax.broadcasted_iota(jnp.int32, (1, 128), 1)
        rows = t_ref[...]
        for i in range(n_blk):
            part = slice(i * capacity, (i + 1) * capacity)
            hit = row == turned[:capacity, i : i + 1]
            row_ref[part, :] = jnp.dot(
                jnp.where(hit, 1.0, 0.0).astype(jnp.bfloat16), rows, preferred_element_type=jnp.float32
            )
            live_ref[i : i + 1, :] = jnp.where(place < n_ref[0, i], 1.0, 0.0)

    return pl.pallas_call(
        kernel,
        out_shape=(
            jax.ShapeDtypeStruct((slots, width), jnp.float32),
            jax.ShapeDtypeStruct((n_blk, 128), jnp.float32),
        ),
        in_specs=[pl.BlockSpec(memory_space=pltpu.SMEM)] + vmem(2),
        out_specs=tuple(vmem(2)),
        scratch_shapes=[pltpu.VMEM((n_blk, 128), jnp.float32)],
        compiler_params=params(4),
        name="prepare",
    )(counts, tokens, row_ids)


def finish(answers, rows, live):
    n_blk, _, width = answers.shape
    capacity = rows.shape[0] // n_blk

    def kernel(g_ref, t_ref, v_ref, out_ref, w_ref):
        for i in range(n_blk):
            w_ref[i : i + 1, :] = g_ref[i, capacity:, :].astype(jnp.float32)
        pieces = w_ref[...]
        exponent = pieces[:, :capacity]
        for k in range(1, 3):
            exponent = exponent + pieces[:, k * capacity : (k + 1) * capacity]
        w_ref[:, :capacity] = jnp.where(v_ref[:, :capacity] > 0.0, jnp.exp(exponent), 0.0)
        turned = jnp.transpose(w_ref[...])
        for i in range(n_blk):
            part = slice(i * capacity, (i + 1) * capacity)
            centre = g_ref[i, :capacity, :].astype(jnp.float32)
            out_ref[0, i] = turned[:capacity, i : i + 1] * (t_ref[part, :] - centre)

    return pl.pallas_call(
        kernel,
        out_shape=jax.ShapeDtypeStruct((1, n_blk, capacity, width), jnp.float32),
        in_specs=vmem(3),
        out_specs=pl.BlockSpec(memory_space=pltpu.VMEM),
        scratch_shapes=[pltpu.VMEM((n_blk, 128), jnp.float32)],
        compiler_params=params(4),
        name="finish",
    )(answers, rows, live)


def local(tokens, centroids, row_ids, alt_ids, counts):
    tok, width = tokens.shape
    slab = centroids.shape[0]
    n_blk = lax.axis_size("blk")
    n_wide = lax.axis_size("wide")
    scaling = score_gain / math.sqrt(width)
    capacity = alt_ids.shape[2]
    pairs = [[k, k + 1] for k in range(0, n_wide, 2)]
    same_core = [list(range(core, n_wide, 2)) for core in range(2)]

    outgoing, near = stage(tokens, centroids, n_blk)
    gathered = exchange(outgoing, "blk")
    sent, kept, base = row_pass(gathered, near, alt_ids[0], row_ids[0], tok, scaling)
    parts = exchange(sent, "blk")
    own_duals, duals, mass = column_pass(gathered, near, parts, kept, base, tok, scaling, slab * n_blk)
    both = lax.all_gather(mass, "wide", axis=0, axis_index_groups=pairs, tiled=True)
    mass = add_up(exchange(spread(both, n_wide // 2), "wide", same_core))
    ids = unpack(parts, n_blk * tok, capacity)
    centres = near[ids[2]]
    sums = ask_scores(gathered, centres, parts, duals, scaling)
    rows, live = prepare(tokens, row_ids[0], counts)
    mass, sums, rows, live = lax.optimization_barrier((mass, sums, rows, live))
    mass = lax.all_gather(mass, "wide", axis=0, axis_index_groups=pairs, tiled=True)
    col_duals, answers = look_up(mass, ids, centres, sums, tok * n_blk * n_wide, n_blk, capacity)
    residuals = finish(exchange(answers, "blk"), rows, live)
    return (own_duals.reshape(tok), col_duals.reshape(slab), residuals)


def solution(mesh):
    in_specs = (
        P(("blk", "wide"), None),
        P("blk", None),
        P(("blk", "wide"), None, None),
        P(("blk", "wide"), None, None),
        P(("blk", "wide"), None),
    )
    out_specs = (P(("blk", "wide")), P("blk"), P(("blk", "wide"), None, None, None))
    return jax.shard_map(local, mesh=mesh, in_specs=in_specs, out_specs=out_specs, check_vma=False)
```

```python
import math

import jax
import jax.numpy as jnp
from jax import lax
from jax.experimental import pallas as pl
from jax.experimental.pallas import tpu as pltpu
from jax.sharding import PartitionSpec as P

score_gain = 3.0
log2e = 1.4426950408889634
dead = -1.0e30


def vmem(n):
    return [pl.BlockSpec(memory_space=pltpu.VMEM)] * n


def load_rows(x_ref, t_ref, n_blk, tok):
    for i in range(n_blk):
        t_ref[i * tok : (i + 1) * tok, :] = x_ref[i, :tok, :]


def exchange(x, axis, groups=None):
    return lax.all_to_all(x, axis, split_axis=0, concat_axis=0, axis_index_groups=groups, tiled=True)


def params(mib):
    return pltpu.CompilerParams(vmem_limit_bytes=mib << 20)


def stage(tokens, centroids, count):
    tok, width = tokens.shape

    def kernel(t_ref, c_ref, copies_ref, t_scr, sem):
        copy = pltpu.make_async_copy(t_ref, t_scr, sem)
        copy.start()
        copy.wait()
        rows = t_scr[...]
        for i in range(count):
            copies_ref[i] = rows

    return pl.pallas_call(
        kernel,
        out_shape=pltpu.VMEM((count, tok, width), tokens.dtype),
        in_specs=[pl.BlockSpec(memory_space=pltpu.HBM)] * 2,
        out_specs=pl.BlockSpec(memory_space=pltpu.VMEM),
        scratch_shapes=[pltpu.VMEM((tok, width), tokens.dtype), pltpu.SemaphoreType.DMA],
        compiler_params=params(56),
        name="stage",
    )(tokens, centroids)


def row_pass(x, centroids, alt_ids, row_ids, tok, scaling):
    n_blk = x.shape[0]
    rows = n_blk * tok
    capacity = alt_ids.shape[1]
    slab, width = centroids.shape
    factor = scaling * log2e
    block = math.gcd(slab, 1024)
    small = math.gcd(slab, 256)
    height = 256

    def kernel(x_ref, c_ref, i_ref, r_ref, out_ref, e_ref, base_ref, t_ref, s_ref, m_ref, a_ref, l_ref):
        load_rows(x_ref, t_ref, n_blk, tok)

        def scores(band, start, size):
            return lax.dot_general(
                t_ref[band, :],
                c_ref[start : start + size, :],
                (((1,), (1,)), ((), ())),
                preferred_element_type=jnp.float32,
            )

        bands = [slice(r, r + height) for r in range(0, rows, height)]
        for band in bands:
            first = jnp.max(scores(band, 0, small), axis=1, keepdims=True)
            base_ref[band, :] = jnp.broadcast_to(first, (height, 128))
        s_ref[...] = jnp.zeros_like(s_ref)
        for start in range(0, slab, block):
            for band in bands:
                s = scores(band, start, block)
                total = s_ref[band, :]
                for g in range(0, block, 128):
                    e = jnp.exp2((s[:, g : g + 128] - base_ref[band, :]) * factor)
                    e_ref[band, start + g : start + g + 128] = e
                    total = total + e
                s_ref[band, :] = total
        base = jnp.transpose(base_ref[...])[:1, :]
        total = jnp.sum(jnp.transpose(s_ref[...]), axis=0, keepdims=True)
        l_ref[...] = base * scaling + jnp.log(total)

        @pl.when(jnp.logical_not(jnp.max(total) < 1.0e15))
        def _():
            m_ref[...] = jnp.full_like(m_ref, dead)
            a_ref[...] = jnp.zeros_like(a_ref)

            def step(j, carry):
                start = pl.multiple_of(j * small, small)
                e_ref[:, pl.ds(start, small)] = jnp.zeros((rows, small), jnp.float32)
                for g in range(0, rows, 256):
                    lanes = slice(g, g + 256)
                    s = lax.dot_general(
                        c_ref[pl.ds(start, small), :],
                        t_ref[lanes, :],
                        (((1,), (1,)), ((), ())),
                        preferred_element_type=jnp.float32,
                    ).reshape(small // 8, 8, 256)
                    old = m_ref[:, lanes]
                    new = jnp.maximum(old, jnp.max(s, axis=0))
                    m_ref[:, lanes] = new
                    part = jnp.sum(jnp.exp2((s - new[None]) * factor), axis=0)
                    a_ref[:, lanes] = a_ref[:, lanes] * jnp.exp2((old - new) * factor) + part
                return carry

            lax.fori_loop(0, slab // small, step, 0)
            m = m_ref[...]
            top = jnp.max(m, axis=0, keepdims=True)
            sums = jnp.sum(a_ref[...] * jnp.exp2((m - top) * factor), axis=0, keepdims=True)
            l_ref[...] = top * scaling + jnp.log(sums)

        lse = l_ref[...]
        ids = i_ref[...]
        line = jnp.concatenate(
            [ids >> 7, ids & 127, r_ref[...], jnp.zeros((n_blk, 128 - 3 * capacity), jnp.int32)], axis=1
        ).astype(jnp.float32)
        for i in range(n_blk):
            out_ref[i, :, :rows] = lse
            out_ref[i, :, rows:] = line[i : i + 1, :]

    return pl.pallas_call(
        kernel,
        out_shape=(
            jax.ShapeDtypeStruct((n_blk, 1, rows + 128), jnp.float32),
            pltpu.VMEM((rows, slab), jnp.float32),
            pltpu.VMEM((rows, 128), jnp.float32),
        ),
        in_specs=vmem(4),
        out_specs=tuple(vmem(3)),
        scratch_shapes=[
            pltpu.VMEM((rows, width), jnp.bfloat16),
            pltpu.VMEM((rows, 128), jnp.float32),
            pltpu.VMEM((8, rows), jnp.float32),
            pltpu.VMEM((8, rows), jnp.float32),
            pltpu.VMEM((1, rows), jnp.float32),
        ],
        compiler_params=params(8),
        name="row_pass",
    )(x, centroids, alt_ids, row_ids)


def unpack(parts, rows, capacity):
    n_blk = parts.shape[0]

    def kernel(p_ref, ids_ref):
        for i in range(n_blk):
            line = p_ref[i, :, rows:].astype(jnp.int32)
            part = slice(i * capacity, (i + 1) * capacity)
            ids_ref[0:1, part] = line[:, :capacity]
            ids_ref[1:2, part] = line[:, capacity : 2 * capacity]
            ids_ref[2:3, part] = line[:, :capacity] * 128 + line[:, capacity : 2 * capacity]

    return pl.pallas_call(
        kernel,
        out_shape=jax.ShapeDtypeStruct((3, n_blk * capacity), jnp.int32),
        in_specs=vmem(1),
        out_specs=pl.BlockSpec(memory_space=pltpu.VMEM),
        compiler_params=params(4),
        name="unpack",
    )(parts)


def column_pass(x, centroids, parts, kept, base, tok, scaling, all_cols):
    n_blk = x.shape[0]
    rows = n_blk * tok
    slab, width = centroids.shape
    block = 256
    factor = scaling * log2e
    lines = slab // 128
    held = math.gcd(lines, 32)
    stride = math.gcd(rows, 256)

    def kernel(x_ref, c_ref, l_ref, e_ref, b_ref, own_ref, dual_ref, mass_ref, t_ref, d_ref, w_ref):
        lse = l_ref[:, 0, :rows]
        top = jnp.max(lse, axis=0, keepdims=True)
        total = jnp.sum(jnp.exp(lse - top), axis=0, keepdims=True)
        dual = math.log(all_cols) - (top + jnp.log(total))
        dual_ref[...] = dual
        position = lax.axis_index("blk")
        own = jnp.zeros((1, tok), jnp.float32)
        for i in range(n_blk):
            own = own + jnp.where(position == i, dual[:, i * tok : (i + 1) * tok], 0.0)
        own_ref[...] = own
        d_ref[...] = jnp.transpose(jnp.broadcast_to(dual * log2e, (128, rows)))
        w_ref[...] = jnp.exp2(b_ref[...] * factor + d_ref[...])

        for first in range(0, lines, held):

            def add(r, sums):
                sums = list(sums)
                start = pl.multiple_of(r * stride, stride)
                for q in range(0, stride, 8):
                    w = w_ref[pl.ds(start + q, 8), :]
                    for g in range(held):
                        k = (first + g) * 128
                        sums[g] = sums[g] + e_ref[pl.ds(start + q, 8), k : k + 128] * w
                return tuple(sums)

            sums = lax.fori_loop(0, rows // stride, add, tuple(jnp.zeros((8, 128), jnp.float32) for _ in range(held)))
            for g in range(held):
                mass_ref[first + g : first + g + 1, :] = jnp.sum(sums[g], axis=0, keepdims=True)

        mass = mass_ref[...]
        sound = jnp.logical_and(jnp.min(mass) > 1.0e-12, jnp.max(mass) < 1.0e12)

        @pl.when(jnp.logical_not(sound))
        def _():
            load_rows(x_ref, t_ref, n_blk, tok)

            def step(k, carry):
                s = lax.dot_general(
                    t_ref[...],
                    c_ref[pl.ds(pl.multiple_of(k * block, block), block), :],
                    (((1,), (1,)), ((), ())),
                    preferred_element_type=jnp.float32,
                )
                d = d_ref[...]
                e = jnp.exp2(s * factor + jnp.concatenate([d] * (block // 128), axis=1))
                part = jnp.sum(e, axis=0, keepdims=True)
                for h in range(block // 128):
                    mass_ref[pl.ds(k * (block // 128) + h, 1), :] = part[:, h * 128 : (h + 1) * 128]
                return carry

            lax.fori_loop(0, slab // block, step, 0)

    return pl.pallas_call(
        kernel,
        out_shape=(
            jax.ShapeDtypeStruct((1, tok), jnp.float32),
            jax.ShapeDtypeStruct((1, rows), jnp.float32),
            jax.ShapeDtypeStruct((lines, 128), jnp.float32),
        ),
        in_specs=vmem(5),
        out_specs=tuple(vmem(3)),
        scratch_shapes=[
            pltpu.VMEM((rows, width), jnp.bfloat16),
            pltpu.VMEM((rows, 128), jnp.float32),
            pltpu.VMEM((rows, 128), jnp.float32),
        ],
        compiler_params=params(8),
        name="column_pass",
    )(x, centroids, parts, kept, base)


def spread(both, copies):
    lines = both.shape[0] // 2
    half = lines // 2

    def kernel(p_ref, out_ref):
        core = lax.rem(lax.axis_index("wide"), 2)
        start = pl.multiple_of(core * half, half)
        part = p_ref[pl.ds(start, half), :] + p_ref[pl.ds(lines + start, half), :]
        for j in range(copies):
            out_ref[j] = part

    return pl.pallas_call(
        kernel,
        out_shape=jax.ShapeDtypeStruct((copies, half, 128), jnp.float32),
        in_specs=vmem(1),
        out_specs=pl.BlockSpec(memory_space=pltpu.VMEM),
        compiler_params=params(4),
        name="spread",
    )(both)


def add_up(parts):
    def kernel(p_ref, out_ref):
        out_ref[...] = jnp.sum(p_ref[...], axis=0)

    return pl.pallas_call(
        kernel,
        out_shape=jax.ShapeDtypeStruct(parts.shape[1:], jnp.float32),
        in_specs=vmem(1),
        out_specs=pl.BlockSpec(memory_space=pltpu.VMEM),
        compiler_params=params(4),
        name="add_up",
    )(parts)


def pieces_of(value):
    rest, pieces = jnp.clip(value, -3.0e38, 3.0e38), []
    for _ in range(3):
        piece = rest.astype(jnp.bfloat16)
        pieces.append(piece)
        rest = rest - piece.astype(jnp.float32)
    return pieces


def ask_scores(x, centres, parts, duals, scaling):
    n_blk, tok, width = x.shape
    rows = n_blk * tok
    capacity = centres.shape[0] // n_blk

    def kernel(x_ref, c_ref, p_ref, d_ref, out_ref, w_ref):
        for i in range(n_blk):
            w_ref[i : i + 1, :] = p_ref[i, :, rows:]
        turned = jnp.transpose(w_ref[...])[2 * capacity : 3 * capacity, :]
        row = lax.broadcasted_iota(jnp.int32, (capacity, tok), 1).astype(jnp.float32)
        lane = lax.broadcasted_iota(jnp.int32, (capacity, 128), 1)
        table = jnp.zeros((capacity, 128), jnp.float32)
        for i in range(n_blk):
            hit = row == turned[:, i : i + 1]
            picked = jnp.dot(
                jnp.where(hit, 1.0, 0.0).astype(jnp.bfloat16), x_ref[i], preferred_element_type=jnp.float32
            )
            centre = c_ref[i * capacity : (i + 1) * capacity, :].astype(jnp.float32)
            score = jnp.sum(picked * centre, axis=1, keepdims=True) * scaling
            dual = jnp.where(hit, d_ref[:, i * tok : (i + 1) * tok], 0.0)
            dual = jnp.sum(dual, axis=1, keepdims=True)
            table = jnp.where(lane == i, score + dual, table)
        table = jnp.transpose(table)
        for i in range(n_blk):
            out_ref[:, i * capacity : (i + 1) * capacity] = table[i : i + 1, :]

    return pl.pallas_call(
        kernel,
        out_shape=jax.ShapeDtypeStruct((1, n_blk * capacity), jnp.float32),
        in_specs=vmem(4),
        out_specs=pl.BlockSpec(memory_space=pltpu.VMEM),
        scratch_shapes=[pltpu.VMEM((n_blk, 128), jnp.float32)],
        compiler_params=params(4),
        name="ask_scores",
    )(x, centres, parts, duals)


def look_up(masses, ids, centres, sums, all_rows, n_blk, capacity):
    lines = masses.shape[0]
    slots = n_blk * capacity

    def kernel(m_ref, i_ref, c_ref, s_ref, dual_ref, out_ref):
        dual = math.log(all_rows) - jnp.log(m_ref[...])
        dual_ref[...] = dual
        line = lax.broadcasted_iota(jnp.int32, (lines, slots), 0)
        pick = jnp.where(line == i_ref[0:1, :], 1.0, 0.0).astype(jnp.bfloat16)
        lane = lax.broadcasted_iota(jnp.int32, (128, slots), 0)
        here = lane == i_ref[1:2, :]
        total = jnp.zeros((128, slots), jnp.float32)
        for piece in pieces_of(dual):
            total = total + lax.dot_general(
                piece, pick, (((0,), (0,)), ((), ())), preferred_element_type=jnp.float32
            )
        total = jnp.sum(jnp.where(here, total, 0.0), axis=0, keepdims=True) + s_ref[...]
        pieces = [piece.astype(jnp.float32) for piece in pieces_of(total)]
        blank = jnp.zeros((1, 128 - 3 * capacity), jnp.float32)
        for i in range(n_blk):
            part = slice(i * capacity, (i + 1) * capacity)
            out_ref[i, :capacity, :] = c_ref[part, :]
            row = jnp.concatenate([piece[:, part] for piece in pieces] + [blank], axis=1)
            out_ref[i, capacity:, :] = row.astype(jnp.bfloat16)

    return pl.pallas_call(
        kernel,
        out_shape=(
            jax.ShapeDtypeStruct((lines, 128), jnp.float32),
            jax.ShapeDtypeStruct((n_blk, capacity + 1, 128), jnp.bfloat16),
        ),
        in_specs=vmem(4),
        out_specs=tuple(vmem(2)),
        compiler_params=params(4),
        name="look_up",
    )(masses, ids, centres, sums)


def prepare(tokens, row_ids, counts):
    n_blk, capacity = row_ids.shape
    slots = n_blk * capacity
    tok, width = tokens.shape

    def kernel(n_ref, t_ref, r_ref, row_ref, live_ref, w_ref):
        w_ref[...] = jnp.zeros_like(w_ref)
        w_ref[:, :capacity] = r_ref[...].astype(jnp.float32)
        turned = jnp.transpose(w_ref[...])
        row = lax.broadcasted_iota(jnp.int32, (capacity, tok), 1).astype(jnp.float32)
        place = lax.broadcasted_iota(jnp.int32, (1, 128), 1)
        rows = t_ref[...]
        for i in range(n_blk):
            part = slice(i * capacity, (i + 1) * capacity)
            hit = row == turned[:capacity, i : i + 1]
            row_ref[part, :] = jnp.dot(
                jnp.where(hit, 1.0, 0.0).astype(jnp.bfloat16), rows, preferred_element_type=jnp.float32
            )
            live_ref[i : i + 1, :] = jnp.where(place < n_ref[0, i], 1.0, 0.0)

    return pl.pallas_call(
        kernel,
        out_shape=(
            jax.ShapeDtypeStruct((slots, width), jnp.float32),
            jax.ShapeDtypeStruct((n_blk, 128), jnp.float32),
        ),
        in_specs=[pl.BlockSpec(memory_space=pltpu.SMEM)] + vmem(2),
        out_specs=tuple(vmem(2)),
        scratch_shapes=[pltpu.VMEM((n_blk, 128), jnp.float32)],
        compiler_params=params(4),
        name="prepare",
    )(counts, tokens, row_ids)


def finish(answers, rows, live):
    n_blk, _, width = answers.shape
    capacity = rows.shape[0] // n_blk

    def kernel(g_ref, t_ref, v_ref, out_ref, w_ref):
        for i in range(n_blk):
            w_ref[i : i + 1, :] = g_ref[i, capacity:, :].astype(jnp.float32)
        pieces = w_ref[...]
        exponent = pieces[:, :capacity]
        for k in range(1, 3):
            exponent = exponent + pieces[:, k * capacity : (k + 1) * capacity]
        w_ref[:, :capacity] = jnp.where(v_ref[:, :capacity] > 0.0, jnp.exp(exponent), 0.0)
        turned = jnp.transpose(w_ref[...])
        for i in range(n_blk):
            part = slice(i * capacity, (i + 1) * capacity)
            centre = g_ref[i, :capacity, :].astype(jnp.float32)
            out_ref[0, i] = turned[:capacity, i : i + 1] * (t_ref[part, :] - centre)

    return pl.pallas_call(
        kernel,
        out_shape=jax.ShapeDtypeStruct((1, n_blk, capacity, width), jnp.float32),
        in_specs=vmem(3),
        out_specs=pl.BlockSpec(memory_space=pltpu.VMEM),
        scratch_shapes=[pltpu.VMEM((n_blk, 128), jnp.float32)],
        compiler_params=params(4),
        name="finish",
    )(answers, rows, live)


def local(tokens, centroids, row_ids, alt_ids, counts):
    tok, width = tokens.shape
    slab = centroids.shape[0]
    n_blk = lax.axis_size("blk")
    n_wide = lax.axis_size("wide")
    scaling = score_gain / math.sqrt(width)
    capacity = alt_ids.shape[2]
    pairs = [[k, k + 1] for k in range(0, n_wide, 2)]
    same_core = [list(range(core, n_wide, 2)) for core in range(2)]

    gathered = exchange(stage(tokens, centroids, n_blk), "blk")
    sent, kept, base = row_pass(gathered, centroids, alt_ids[0], row_ids[0], tok, scaling)
    parts = exchange(sent, "blk")
    own_duals, duals, mass = column_pass(gathered, centroids, parts, kept, base, tok, scaling, slab * n_blk)
    both = lax.all_gather(mass, "wide", axis=0, axis_index_groups=pairs, tiled=True)
    mass = add_up(exchange(spread(both, n_wide // 2), "wide", same_core))
    ids = unpack(parts, n_blk * tok, capacity)
    centres = centroids[ids[2]]
    sums = ask_scores(gathered, centres, parts, duals, scaling)
    rows, live = prepare(tokens, row_ids[0], counts)
    mass, sums, rows, live = lax.optimization_barrier((mass, sums, rows, live))
    mass = lax.all_gather(mass, "wide", axis=0, axis_index_groups=pairs, tiled=True)
    col_duals, answers = look_up(mass, ids, centres, sums, tok * n_blk * n_wide, n_blk, capacity)
    residuals = finish(exchange(answers, "blk"), rows, live)
    return (own_duals.reshape(tok), col_duals.reshape(slab), residuals)


def solution(mesh):
    in_specs = (
        P(("blk", "wide"), None),
        P("blk", None),
        P(("blk", "wide"), None, None),
        P(("blk", "wide"), None, None),
        P(("blk", "wide"), None),
    )
    out_specs = (P(("blk", "wide")), P("blk"), P(("blk", "wide"), None, None, None))
    return jax.shard_map(local, mesh=mesh, in_specs=in_specs, out_specs=out_specs, check_vma=False)
```

```python
import math

import jax
import jax.numpy as jnp
from jax import lax
from jax.experimental import pallas as pl
from jax.experimental.pallas import tpu as pltpu
from jax.sharding import PartitionSpec as P

score_gain = 3.0
log2e = 1.4426950408889634
dead = -1.0e30


def vmem(n):
    return [pl.BlockSpec(memory_space=pltpu.VMEM)] * n


def load_rows(x_ref, t_ref, n_blk, tok):
    for i in range(n_blk):
        t_ref[i * tok : (i + 1) * tok, :] = x_ref[i, :tok, :]


def exchange(x, axis, groups=None):
    return lax.all_to_all(x, axis, split_axis=0, concat_axis=0, axis_index_groups=groups, tiled=True)


def params(mib):
    return pltpu.CompilerParams(vmem_limit_bytes=mib << 20)


def stage(tokens, centroids, count):
    tok, width = tokens.shape

    def kernel(t_ref, c_ref, copies_ref, t_scr, sem):
        copy = pltpu.make_async_copy(t_ref, t_scr, sem)
        copy.start()
        copy.wait()
        rows = t_scr[...]
        for i in range(count):
            copies_ref[i] = rows

    return pl.pallas_call(
        kernel,
        out_shape=pltpu.VMEM((count, tok, width), tokens.dtype),
        in_specs=[pl.BlockSpec(memory_space=pltpu.HBM)] * 2,
        out_specs=pl.BlockSpec(memory_space=pltpu.VMEM),
        scratch_shapes=[pltpu.VMEM((tok, width), tokens.dtype), pltpu.SemaphoreType.DMA],
        compiler_params=params(56),
        name="stage",
    )(tokens, centroids)


def row_pass(x, centroids, alt_ids, row_ids, tok, scaling):
    n_blk = x.shape[0]
    rows = n_blk * tok
    capacity = alt_ids.shape[1]
    slab, width = centroids.shape
    factor = scaling * log2e
    block = math.gcd(slab, 1024)
    small = math.gcd(slab, 256)
    height = 256

    def kernel(x_ref, c_ref, i_ref, r_ref, out_ref, e_ref, base_ref, t_ref, s_ref, m_ref, a_ref, l_ref):
        load_rows(x_ref, t_ref, n_blk, tok)

        def scores(band, start, size):
            return lax.dot_general(
                t_ref[band, :],
                c_ref[start : start + size, :],
                (((1,), (1,)), ((), ())),
                preferred_element_type=jnp.float32,
            )

        bands = [slice(r, r + height) for r in range(0, rows, height)]
        for band in bands:
            first = jnp.max(scores(band, 0, small), axis=1, keepdims=True)
            base_ref[band, :] = jnp.broadcast_to(first, (height, 128))
        s_ref[...] = jnp.zeros_like(s_ref)
        for start in range(0, slab, block):
            for band in bands:
                s = scores(band, start, block)
                total = s_ref[band, :]
                for g in range(0, block, 128):
                    e = jnp.exp2((s[:, g : g + 128] - base_ref[band, :]) * factor)
                    e_ref[band, start + g : start + g + 128] = e
                    total = total + e
                s_ref[band, :] = total
        base = jnp.transpose(base_ref[...])[:1, :]
        total = jnp.sum(jnp.transpose(s_ref[...]), axis=0, keepdims=True)
        l_ref[...] = base * scaling + jnp.log(total)

        @pl.when(jnp.logical_not(jnp.max(total) < 1.0e15))
        def _():
            m_ref[...] = jnp.full_like(m_ref, dead)
            a_ref[...] = jnp.zeros_like(a_ref)

            def step(j, carry):
                start = pl.multiple_of(j * small, small)
                e_ref[:, pl.ds(start, small)] = jnp.zeros((rows, small), jnp.float32)
                for g in range(0, rows, 256):
                    lanes = slice(g, g + 256)
                    s = lax.dot_general(
                        c_ref[pl.ds(start, small), :],
                        t_ref[lanes, :],
                        (((1,), (1,)), ((), ())),
                        preferred_element_type=jnp.float32,
                    ).reshape(small // 8, 8, 256)
                    old = m_ref[:, lanes]
                    new = jnp.maximum(old, jnp.max(s, axis=0))
                    m_ref[:, lanes] = new
                    part = jnp.sum(jnp.exp2((s - new[None]) * factor), axis=0)
                    a_ref[:, lanes] = a_ref[:, lanes] * jnp.exp2((old - new) * factor) + part
                return carry

            lax.fori_loop(0, slab // small, step, 0)
            m = m_ref[...]
            top = jnp.max(m, axis=0, keepdims=True)
            sums = jnp.sum(a_ref[...] * jnp.exp2((m - top) * factor), axis=0, keepdims=True)
            l_ref[...] = top * scaling + jnp.log(sums)

        lse = l_ref[...]
        ids = i_ref[...]
        line = jnp.concatenate(
            [ids >> 7, ids & 127, r_ref[...], jnp.zeros((n_blk, 128 - 3 * capacity), jnp.int32)], axis=1
        ).astype(jnp.float32)
        for i in range(n_blk):
            out_ref[i, :, :rows] = lse
            out_ref[i, :, rows:] = line[i : i + 1, :]

    return pl.pallas_call(
        kernel,
        out_shape=(
            jax.ShapeDtypeStruct((n_blk, 1, rows + 128), jnp.float32),
            pltpu.VMEM((rows, slab), jnp.float32),
            pltpu.VMEM((rows, 128), jnp.float32),
        ),
        in_specs=vmem(4),
        out_specs=tuple(vmem(3)),
        scratch_shapes=[
            pltpu.VMEM((rows, width), jnp.bfloat16),
            pltpu.VMEM((rows, 128), jnp.float32),
            pltpu.VMEM((8, rows), jnp.float32),
            pltpu.VMEM((8, rows), jnp.float32),
            pltpu.VMEM((1, rows), jnp.float32),
        ],
        compiler_params=params(8),
        name="row_pass",
    )(x, centroids, alt_ids, row_ids)


def unpack(parts, rows, lines, capacity):
    n_blk = parts.shape[0]
    slots = n_blk * capacity

    def kernel(p_ref, ids_ref, pick_ref, here_ref, h_ref, l_ref):
        for i in range(n_blk):
            line = p_ref[i, :, rows:].astype(jnp.int32)
            part = slice(i * capacity, (i + 1) * capacity)
            h_ref[:, part] = line[:, :capacity]
            l_ref[:, part] = line[:, capacity : 2 * capacity]
        ids_ref[...] = h_ref[...] * 128 + l_ref[...]
        line = lax.broadcasted_iota(jnp.int32, (lines, slots), 0)
        pick_ref[...] = jnp.where(line == h_ref[...], 1.0, 0.0).astype(jnp.bfloat16)
        lane = lax.broadcasted_iota(jnp.int32, (128, slots), 0)
        here_ref[...] = jnp.where(lane == l_ref[...], 1.0, 0.0)

    return pl.pallas_call(
        kernel,
        out_shape=(
            jax.ShapeDtypeStruct((1, slots), jnp.int32),
            jax.ShapeDtypeStruct((lines, slots), jnp.bfloat16),
            jax.ShapeDtypeStruct((128, slots), jnp.float32),
        ),
        in_specs=vmem(1),
        out_specs=tuple(vmem(3)),
        scratch_shapes=[pltpu.VMEM((1, slots), jnp.int32)] * 2,
        compiler_params=params(4),
        name="unpack",
    )(parts)


def column_pass(x, centroids, parts, kept, base, tok, scaling, all_cols):
    n_blk = x.shape[0]
    rows = n_blk * tok
    slab, width = centroids.shape
    block = 256
    factor = scaling * log2e
    lines = slab // 128
    held = math.gcd(lines, 32)
    stride = math.gcd(rows, 256)

    def kernel(x_ref, c_ref, l_ref, e_ref, b_ref, own_ref, dual_ref, mass_ref, t_ref, d_ref, w_ref):
        lse = l_ref[:, 0, :rows]
        top = jnp.max(lse, axis=0, keepdims=True)
        total = jnp.sum(jnp.exp(lse - top), axis=0, keepdims=True)
        dual = math.log(all_cols) - (top + jnp.log(total))
        dual_ref[...] = dual
        position = lax.axis_index("blk")
        own = jnp.zeros((1, tok), jnp.float32)
        for i in range(n_blk):
            own = own + jnp.where(position == i, dual[:, i * tok : (i + 1) * tok], 0.0)
        own_ref[...] = own
        d_ref[...] = jnp.transpose(jnp.broadcast_to(dual * log2e, (128, rows)))
        w_ref[...] = jnp.exp2(b_ref[...] * factor + d_ref[...])

        for first in range(0, lines, held):

            def add(r, sums):
                sums = list(sums)
                start = pl.multiple_of(r * stride, stride)
                for q in range(0, stride, 8):
                    w = w_ref[pl.ds(start + q, 8), :]
                    for g in range(held):
                        k = (first + g) * 128
                        sums[g] = sums[g] + e_ref[pl.ds(start + q, 8), k : k + 128] * w
                return tuple(sums)

            sums = lax.fori_loop(0, rows // stride, add, tuple(jnp.zeros((8, 128), jnp.float32) for _ in range(held)))
            for g in range(held):
                mass_ref[first + g : first + g + 1, :] = jnp.sum(sums[g], axis=0, keepdims=True)

        mass = mass_ref[...]
        sound = jnp.logical_and(jnp.min(mass) > 1.0e-12, jnp.max(mass) < 1.0e12)

        @pl.when(jnp.logical_not(sound))
        def _():
            load_rows(x_ref, t_ref, n_blk, tok)

            def step(k, carry):
                s = lax.dot_general(
                    t_ref[...],
                    c_ref[pl.ds(pl.multiple_of(k * block, block), block), :],
                    (((1,), (1,)), ((), ())),
                    preferred_element_type=jnp.float32,
                )
                d = d_ref[...]
                e = jnp.exp2(s * factor + jnp.concatenate([d] * (block // 128), axis=1))
                part = jnp.sum(e, axis=0, keepdims=True)
                for h in range(block // 128):
                    mass_ref[pl.ds(k * (block // 128) + h, 1), :] = part[:, h * 128 : (h + 1) * 128]
                return carry

            lax.fori_loop(0, slab // block, step, 0)

    return pl.pallas_call(
        kernel,
        out_shape=(
            jax.ShapeDtypeStruct((1, tok), jnp.float32),
            jax.ShapeDtypeStruct((1, rows), jnp.float32),
            jax.ShapeDtypeStruct((lines, 128), jnp.float32),
        ),
        in_specs=vmem(5),
        out_specs=tuple(vmem(3)),
        scratch_shapes=[
            pltpu.VMEM((rows, width), jnp.bfloat16),
            pltpu.VMEM((rows, 128), jnp.float32),
            pltpu.VMEM((rows, 128), jnp.float32),
        ],
        compiler_params=params(8),
        name="column_pass",
    )(x, centroids, parts, kept, base)


def spread(both, copies):
    lines = both.shape[0] // 2
    half = lines // 2
    group = math.gcd(copies, 4)

    def kernel(p_ref, out_ref, part_ref, sems):
        core = lax.rem(lax.axis_index("wide"), 2)
        start = pl.multiple_of(core * half, half)
        part = p_ref[pl.ds(start, half), :] + p_ref[pl.ds(lines + start, half), :]
        for j in range(group):
            part_ref[j] = part
        moves = [
            pltpu.make_async_copy(part_ref, out_ref.at[pl.ds(j * group, group)], sems.at[j])
            for j in range(copies // group)
        ]
        for move in moves:
            move.start()
        for move in moves:
            move.wait()

    return pl.pallas_call(
        kernel,
        out_shape=jax.ShapeDtypeStruct((copies, half, 128), jnp.float32),
        in_specs=vmem(1),
        out_specs=pl.BlockSpec(memory_space=pltpu.HBM),
        scratch_shapes=[
            pltpu.VMEM((group, half, 128), jnp.float32),
            pltpu.SemaphoreType.DMA((copies // group,)),
        ],
        compiler_params=params(4),
        name="spread",
    )(both)


def add_up(parts):
    def kernel(p_ref, out_ref):
        out_ref[...] = jnp.sum(p_ref[...], axis=0)

    return pl.pallas_call(
        kernel,
        out_shape=jax.ShapeDtypeStruct(parts.shape[1:], jnp.float32),
        in_specs=vmem(1),
        out_specs=pl.BlockSpec(memory_space=pltpu.VMEM),
        compiler_params=params(4),
        name="add_up",
    )(parts)


def pieces_of(value):
    rest, pieces = jnp.clip(value, -3.0e38, 3.0e38), []
    for _ in range(3):
        piece = rest.astype(jnp.bfloat16)
        pieces.append(piece)
        rest = rest - piece.astype(jnp.float32)
    return pieces


def ask_scores(x, centres, parts, duals, scaling):
    n_blk, tok, width = x.shape
    rows = n_blk * tok
    capacity = centres.shape[0] // n_blk

    def kernel(x_ref, c_ref, p_ref, d_ref, out_ref, w_ref):
        for i in range(n_blk):
            w_ref[i : i + 1, :] = p_ref[i, :, rows:]
        turned = jnp.transpose(w_ref[...])[2 * capacity : 3 * capacity, :]
        row = lax.broadcasted_iota(jnp.int32, (capacity, tok), 1).astype(jnp.float32)
        lane = lax.broadcasted_iota(jnp.int32, (capacity, 128), 1)
        table = jnp.zeros((capacity, 128), jnp.float32)
        for i in range(n_blk):
            hit = row == turned[:, i : i + 1]
            picked = jnp.dot(
                jnp.where(hit, 1.0, 0.0).astype(jnp.bfloat16), x_ref[i], preferred_element_type=jnp.float32
            )
            centre = c_ref[i * capacity : (i + 1) * capacity, :].astype(jnp.float32)
            score = jnp.sum(picked * centre, axis=1, keepdims=True) * scaling
            dual = jnp.where(hit, d_ref[:, i * tok : (i + 1) * tok], 0.0)
            dual = jnp.sum(dual, axis=1, keepdims=True)
            table = jnp.where(lane == i, score + dual, table)
        table = jnp.transpose(table)
        for i in range(n_blk):
            out_ref[:, i * capacity : (i + 1) * capacity] = table[i : i + 1, :]

    return pl.pallas_call(
        kernel,
        out_shape=jax.ShapeDtypeStruct((1, n_blk * capacity), jnp.float32),
        in_specs=vmem(4),
        out_specs=pl.BlockSpec(memory_space=pltpu.VMEM),
        scratch_shapes=[pltpu.VMEM((n_blk, 128), jnp.float32)],
        compiler_params=params(4),
        name="ask_scores",
    )(x, centres, parts, duals)


def look_up(masses, pick, here, centres, sums, all_rows, n_blk, capacity):
    lines = masses.shape[0]
    slots = n_blk * capacity

    def kernel(m_ref, k_ref, h_ref, c_ref, s_ref, dual_ref, out_ref):
        dual = math.log(all_rows) - jnp.log(m_ref[...])
        dual_ref[...] = dual
        picks = k_ref[...]
        total = jnp.zeros((128, slots), jnp.float32)
        for piece in pieces_of(dual):
            total = total + lax.dot_general(
                piece, picks, (((0,), (0,)), ((), ())), preferred_element_type=jnp.float32
            )
        total = jnp.sum(jnp.where(h_ref[...] > 0.0, total, 0.0), axis=0, keepdims=True) + s_ref[...]
        pieces = [piece.astype(jnp.float32) for piece in pieces_of(total)]
        blank = jnp.zeros((1, 128 - 3 * capacity), jnp.float32)
        for i in range(n_blk):
            part = slice(i * capacity, (i + 1) * capacity)
            out_ref[i, :capacity, :] = c_ref[part, :]
            row = jnp.concatenate([piece[:, part] for piece in pieces] + [blank], axis=1)
            out_ref[i, capacity:, :] = row.astype(jnp.bfloat16)

    return pl.pallas_call(
        kernel,
        out_shape=(
            jax.ShapeDtypeStruct((lines, 128), jnp.float32),
            jax.ShapeDtypeStruct((n_blk, capacity + 1, 128), jnp.bfloat16),
        ),
        in_specs=vmem(5),
        out_specs=tuple(vmem(2)),
        compiler_params=params(4),
        name="look_up",
    )(masses, pick, here, centres, sums)


def prepare(tokens, row_ids, counts):
    n_blk, capacity = row_ids.shape
    slots = n_blk * capacity
    tok, width = tokens.shape

    def kernel(n_ref, t_ref, r_ref, row_ref, live_ref, w_ref):
        w_ref[...] = jnp.zeros_like(w_ref)
        w_ref[:, :capacity] = r_ref[...].astype(jnp.float32)
        turned = jnp.transpose(w_ref[...])
        row = lax.broadcasted_iota(jnp.int32, (capacity, tok), 1).astype(jnp.float32)
        place = lax.broadcasted_iota(jnp.int32, (1, 128), 1)
        rows = t_ref[...]
        for i in range(n_blk):
            part = slice(i * capacity, (i + 1) * capacity)
            hit = row == turned[:capacity, i : i + 1]
            row_ref[part, :] = jnp.dot(
                jnp.where(hit, 1.0, 0.0).astype(jnp.bfloat16), rows, preferred_element_type=jnp.float32
            )
            live_ref[i : i + 1, :] = jnp.where(place < n_ref[0, i], 1.0, 0.0)

    return pl.pallas_call(
        kernel,
        out_shape=(
            jax.ShapeDtypeStruct((slots, width), jnp.float32),
            jax.ShapeDtypeStruct((n_blk, 128), jnp.float32),
        ),
        in_specs=[pl.BlockSpec(memory_space=pltpu.SMEM)] + vmem(2),
        out_specs=tuple(vmem(2)),
        scratch_shapes=[pltpu.VMEM((n_blk, 128), jnp.float32)],
        compiler_params=params(4),
        name="prepare",
    )(counts, tokens, row_ids)


def finish(answers, rows, live):
    n_blk, _, width = answers.shape
    capacity = rows.shape[0] // n_blk
    batch = n_blk // 4

    def kernel(g_ref, t_ref, v_ref, out_ref, w_ref, o_ref, sems):
        for i in range(n_blk):
            w_ref[i : i + 1, :] = g_ref[i, capacity:, :].astype(jnp.float32)
        pieces = w_ref[...]
        exponent = pieces[:, :capacity]
        for k in range(1, 3):
            exponent = exponent + pieces[:, k * capacity : (k + 1) * capacity]
        w_ref[:, :capacity] = jnp.where(v_ref[:, :capacity] > 0.0, jnp.exp(exponent), 0.0)
        turned = jnp.transpose(w_ref[...])
        moves = []
        for i in range(n_blk):
            part = slice(i * capacity, (i + 1) * capacity)
            centre = g_ref[i, :capacity, :].astype(jnp.float32)
            o_ref[i] = turned[:capacity, i : i + 1] * (t_ref[part, :] - centre)
            if (i + 1) % batch == 0:
                first = i + 1 - batch
                move = pltpu.make_async_copy(
                    o_ref.at[pl.ds(first, batch)], out_ref.at[0, pl.ds(first, batch)], sems.at[len(moves)]
                )
                move.start()
                moves.append(move)
        for move in moves:
            move.wait()

    return pl.pallas_call(
        kernel,
        out_shape=jax.ShapeDtypeStruct((1, n_blk, capacity, width), jnp.float32),
        in_specs=vmem(3),
        out_specs=pl.BlockSpec(memory_space=pltpu.HBM),
        scratch_shapes=[
            pltpu.VMEM((n_blk, 128), jnp.float32),
            pltpu.VMEM((n_blk, capacity, width), jnp.float32),
            pltpu.SemaphoreType.DMA((4,)),
        ],
        compiler_params=params(4),
        name="finish",
    )(answers, rows, live)


def local(tokens, centroids, row_ids, alt_ids, counts):
    tok, width = tokens.shape
    slab = centroids.shape[0]
    n_blk = lax.axis_size("blk")
    n_wide = lax.axis_size("wide")
    scaling = score_gain / math.sqrt(width)
    capacity = alt_ids.shape[2]
    pairs = [[k, k + 1] for k in range(0, n_wide, 2)]
    same_core = [list(range(core, n_wide, 2)) for core in range(2)]

    gathered = exchange(stage(tokens, centroids, n_blk), "blk")
    sent, kept, base = row_pass(gathered, centroids, alt_ids[0], row_ids[0], tok, scaling)
    parts = exchange(sent, "blk")
    own_duals, duals, mass = column_pass(gathered, centroids, parts, kept, base, tok, scaling, slab * n_blk)
    both = lax.all_gather(mass, "wide", axis=0, axis_index_groups=pairs, tiled=True)
    mass = add_up(exchange(spread(both, n_wide // 2), "wide", same_core))
    ids, pick, here = unpack(parts, n_blk * tok, slab // 128, capacity)
    centres = centroids[ids[0]]
    sums = ask_scores(gathered, centres, parts, duals, scaling)
    rows, live = prepare(tokens, row_ids[0], counts)
    mass, sums, rows, live = lax.optimization_barrier((mass, sums, rows, live))
    mass = lax.all_gather(mass, "wide", axis=0, axis_index_groups=pairs, tiled=True)
    col_duals, answers = look_up(mass, pick, here, centres, sums, tok * n_blk * n_wide, n_blk, capacity)
    residuals = finish(exchange(answers, "blk"), rows, live)
    return (own_duals.reshape(tok), col_duals.reshape(slab), residuals)


def solution(mesh):
    in_specs = (
        P(("blk", "wide"), None),
        P("blk", None),
        P(("blk", "wide"), None, None),
        P(("blk", "wide"), None, None),
        P(("blk", "wide"), None),
    )
    out_specs = (P(("blk", "wide")), P("blk"), P(("blk", "wide"), None, None, None))
    return jax.shard_map(local, mesh=mesh, in_specs=in_specs, out_specs=out_specs, check_vma=False)
```

```python
import math

import jax
import jax.numpy as jnp
from jax import lax
from jax.experimental import pallas as pl
from jax.experimental.pallas import tpu as pltpu
from jax.sharding import PartitionSpec as P

score_gain = 3.0
log2e = 1.4426950408889634
dead = -1.0e30


def vmem(n):
    return [pl.BlockSpec(memory_space=pltpu.VMEM)] * n


def load_rows(x_ref, t_ref, n_blk, tok):
    for i in range(n_blk):
        t_ref[i * tok : (i + 1) * tok, :] = x_ref[i, :tok, :]


def exchange(x, axis, groups=None):
    return lax.all_to_all(x, axis, split_axis=0, concat_axis=0, axis_index_groups=groups, tiled=True)


def params(mib):
    return pltpu.CompilerParams(vmem_limit_bytes=mib << 20)


def stage(tokens, centroids, count):
    tok, width = tokens.shape

    def kernel(t_ref, c_ref, copies_ref, t_scr, sem):
        copy = pltpu.make_async_copy(t_ref, t_scr, sem)
        copy.start()
        copy.wait()
        rows = t_scr[...]
        for i in range(count):
            copies_ref[i] = rows

    return pl.pallas_call(
        kernel,
        out_shape=pltpu.VMEM((count, tok, width), tokens.dtype),
        in_specs=[pl.BlockSpec(memory_space=pltpu.HBM)] * 2,
        out_specs=pl.BlockSpec(memory_space=pltpu.VMEM),
        scratch_shapes=[pltpu.VMEM((tok, width), tokens.dtype), pltpu.SemaphoreType.DMA],
        compiler_params=params(56),
        name="stage",
    )(tokens, centroids)


def row_pass(x, centroids, alt_ids, row_ids, tok, scaling):
    n_blk = x.shape[0]
    rows = n_blk * tok
    capacity = alt_ids.shape[1]
    slab, width = centroids.shape
    factor = scaling * log2e
    block = math.gcd(slab, 1024)
    small = math.gcd(slab, 256)
    height = 256

    def kernel(x_ref, c_ref, i_ref, r_ref, out_ref, e_ref, base_ref, t_ref, s_ref, m_ref, a_ref, l_ref):
        load_rows(x_ref, t_ref, n_blk, tok)

        def scores(band, start, size):
            return lax.dot_general(
                t_ref[band, :],
                c_ref[start : start + size, :],
                (((1,), (1,)), ((), ())),
                preferred_element_type=jnp.float32,
            )

        bands = [slice(r, r + height) for r in range(0, rows, height)]
        for band in bands:
            first = jnp.max(scores(band, 0, small), axis=1, keepdims=True)
            base_ref[band, :] = jnp.broadcast_to(first, (height, 128))
        s_ref[...] = jnp.zeros_like(s_ref)
        for start in range(0, slab, block):
            for band in bands:
                s = scores(band, start, block)
                total = s_ref[band, :]
                for g in range(0, block, 128):
                    e = jnp.exp2((s[:, g : g + 128] - base_ref[band, :]) * factor)
                    e_ref[band, start + g : start + g + 128] = e
                    total = total + e
                s_ref[band, :] = total
        base = jnp.transpose(base_ref[...])[:1, :]
        total = jnp.sum(jnp.transpose(s_ref[...]), axis=0, keepdims=True)
        l_ref[...] = base * scaling + jnp.log(total)

        @pl.when(jnp.logical_not(jnp.max(total) < 1.0e15))
        def _():
            m_ref[...] = jnp.full_like(m_ref, dead)
            a_ref[...] = jnp.zeros_like(a_ref)

            def step(j, carry):
                start = pl.multiple_of(j * small, small)
                e_ref[:, pl.ds(start, small)] = jnp.zeros((rows, small), jnp.float32)
                for g in range(0, rows, 256):
                    lanes = slice(g, g + 256)
                    s = lax.dot_general(
                        c_ref[pl.ds(start, small), :],
                        t_ref[lanes, :],
                        (((1,), (1,)), ((), ())),
                        preferred_element_type=jnp.float32,
                    ).reshape(small // 8, 8, 256)
                    old = m_ref[:, lanes]
                    new = jnp.maximum(old, jnp.max(s, axis=0))
                    m_ref[:, lanes] = new
                    part = jnp.sum(jnp.exp2((s - new[None]) * factor), axis=0)
                    a_ref[:, lanes] = a_ref[:, lanes] * jnp.exp2((old - new) * factor) + part
                return carry

            lax.fori_loop(0, slab // small, step, 0)
            m = m_ref[...]
            top = jnp.max(m, axis=0, keepdims=True)
            sums = jnp.sum(a_ref[...] * jnp.exp2((m - top) * factor), axis=0, keepdims=True)
            l_ref[...] = top * scaling + jnp.log(sums)

        lse = l_ref[...]
        ids = i_ref[...]
        line = jnp.concatenate(
            [ids >> 7, ids & 127, r_ref[...], jnp.zeros((n_blk, 128 - 3 * capacity), jnp.int32)], axis=1
        ).astype(jnp.float32)
        groups = [lse[:, g : g + 128] for g in range(0, rows, 128)]
        blank = jnp.zeros((8 - len(groups) - 1, 128), jnp.float32)
        for i in range(n_blk):
            out_ref[i] = jnp.concatenate(groups + [line[i : i + 1, :], blank], axis=0)

    return pl.pallas_call(
        kernel,
        out_shape=(
            jax.ShapeDtypeStruct((n_blk, 8, 128), jnp.float32),
            pltpu.VMEM((rows, slab), jnp.float32),
            pltpu.VMEM((rows, 128), jnp.float32),
        ),
        in_specs=vmem(4),
        out_specs=tuple(vmem(3)),
        scratch_shapes=[
            pltpu.VMEM((rows, width), jnp.bfloat16),
            pltpu.VMEM((rows, 128), jnp.float32),
            pltpu.VMEM((8, rows), jnp.float32),
            pltpu.VMEM((8, rows), jnp.float32),
            pltpu.VMEM((1, rows), jnp.float32),
        ],
        compiler_params=params(8),
        name="row_pass",
    )(x, centroids, alt_ids, row_ids)


def unpack(parts, rows, capacity):
    n_blk = parts.shape[0]

    def kernel(p_ref, ids_ref):
        for i in range(n_blk):
            line = p_ref[i, rows // 128 : rows // 128 + 1, :].astype(jnp.int32)
            part = slice(i * capacity, (i + 1) * capacity)
            ids_ref[0:1, part] = line[:, :capacity]
            ids_ref[1:2, part] = line[:, capacity : 2 * capacity]
            ids_ref[2:3, part] = line[:, :capacity] * 128 + line[:, capacity : 2 * capacity]

    return pl.pallas_call(
        kernel,
        out_shape=jax.ShapeDtypeStruct((3, n_blk * capacity), jnp.int32),
        in_specs=vmem(1),
        out_specs=pl.BlockSpec(memory_space=pltpu.VMEM),
        compiler_params=params(4),
        name="unpack",
    )(parts)


def column_pass(x, centroids, parts, kept, base, tok, scaling, all_cols):
    n_blk = x.shape[0]
    rows = n_blk * tok
    slab, width = centroids.shape
    block = 256
    factor = scaling * log2e
    lines = slab // 128
    held = math.gcd(lines, 32)
    stride = math.gcd(rows, 256)

    def kernel(x_ref, c_ref, l_ref, e_ref, b_ref, own_ref, dual_ref, mass_ref, t_ref, d_ref, w_ref):
        lse = l_ref[...]
        top = jnp.max(lse, axis=0)
        total = jnp.sum(jnp.exp(lse - top[None]), axis=0)
        parts_of = math.log(all_cols) - (top + jnp.log(total))
        for g in range(rows // 128):
            dual_ref[:, g * 128 : (g + 1) * 128] = parts_of[g : g + 1, :]
        dual = dual_ref[...]
        position = lax.axis_index("blk")
        own = jnp.zeros((1, tok), jnp.float32)
        for i in range(n_blk):
            own = own + jnp.where(position == i, dual[:, i * tok : (i + 1) * tok], 0.0)
        own_ref[...] = own
        d_ref[...] = jnp.transpose(jnp.broadcast_to(dual * log2e, (128, rows)))
        w_ref[...] = jnp.exp2(b_ref[...] * factor + d_ref[...])

        for first in range(0, lines, held):

            def add(r, sums):
                sums = list(sums)
                start = pl.multiple_of(r * stride, stride)
                for q in range(0, stride, 8):
                    w = w_ref[pl.ds(start + q, 8), :]
                    for g in range(held):
                        k = (first + g) * 128
                        sums[g] = sums[g] + e_ref[pl.ds(start + q, 8), k : k + 128] * w
                return tuple(sums)

            sums = lax.fori_loop(0, rows // stride, add, tuple(jnp.zeros((8, 128), jnp.float32) for _ in range(held)))
            for g in range(held):
                mass_ref[first + g : first + g + 1, :] = jnp.sum(sums[g], axis=0, keepdims=True)

        mass = mass_ref[...]
        sound = jnp.logical_and(jnp.min(mass) > 1.0e-12, jnp.max(mass) < 1.0e12)

        @pl.when(jnp.logical_not(sound))
        def _():
            load_rows(x_ref, t_ref, n_blk, tok)

            def step(k, carry):
                s = lax.dot_general(
                    t_ref[...],
                    c_ref[pl.ds(pl.multiple_of(k * block, block), block), :],
                    (((1,), (1,)), ((), ())),
                    preferred_element_type=jnp.float32,
                )
                d = d_ref[...]
                e = jnp.exp2(s * factor + jnp.concatenate([d] * (block // 128), axis=1))
                part = jnp.sum(e, axis=0, keepdims=True)
                for h in range(block // 128):
                    mass_ref[pl.ds(k * (block // 128) + h, 1), :] = part[:, h * 128 : (h + 1) * 128]
                return carry

            lax.fori_loop(0, slab // block, step, 0)

    return pl.pallas_call(
        kernel,
        out_shape=(
            jax.ShapeDtypeStruct((1, tok), jnp.float32),
            jax.ShapeDtypeStruct((1, rows), jnp.float32),
            jax.ShapeDtypeStruct((lines, 128), jnp.float32),
        ),
        in_specs=vmem(5),
        out_specs=tuple(vmem(3)),
        scratch_shapes=[
            pltpu.VMEM((rows, width), jnp.bfloat16),
            pltpu.VMEM((rows, 128), jnp.float32),
            pltpu.VMEM((rows, 128), jnp.float32),
        ],
        compiler_params=params(8),
        name="column_pass",
    )(x, centroids, parts, kept, base)


def spread(both, copies):
    lines = both.shape[0] // 2
    half = lines // 2

    def kernel(p_ref, out_ref):
        core = lax.rem(lax.axis_index("wide"), 2)
        start = pl.multiple_of(core * half, half)
        part = p_ref[pl.ds(start, half), :] + p_ref[pl.ds(lines + start, half), :]
        for j in range(copies):
            out_ref[j] = part

    return pl.pallas_call(
        kernel,
        out_shape=jax.ShapeDtypeStruct((copies, half, 128), jnp.float32),
        in_specs=vmem(1),
        out_specs=pl.BlockSpec(memory_space=pltpu.VMEM),
        compiler_params=params(4),
        name="spread",
    )(both)


def add_up(parts):
    def kernel(p_ref, out_ref):
        out_ref[...] = jnp.sum(p_ref[...], axis=0)

    return pl.pallas_call(
        kernel,
        out_shape=jax.ShapeDtypeStruct(parts.shape[1:], jnp.float32),
        in_specs=vmem(1),
        out_specs=pl.BlockSpec(memory_space=pltpu.VMEM),
        compiler_params=params(4),
        name="add_up",
    )(parts)


def pieces_of(value):
    rest, pieces = jnp.clip(value, -3.0e38, 3.0e38), []
    for _ in range(3):
        piece = rest.astype(jnp.bfloat16)
        pieces.append(piece)
        rest = rest - piece.astype(jnp.float32)
    return pieces


def ask_scores(x, centres, parts, duals, scaling):
    n_blk, tok, width = x.shape
    rows = n_blk * tok
    capacity = centres.shape[0] // n_blk

    def kernel(x_ref, c_ref, p_ref, d_ref, out_ref, w_ref):
        for i in range(n_blk):
            w_ref[i : i + 1, :] = p_ref[i, rows // 128 : rows // 128 + 1, :]
        turned = jnp.transpose(w_ref[...])[2 * capacity : 3 * capacity, :]
        row = lax.broadcasted_iota(jnp.int32, (capacity, tok), 1).astype(jnp.float32)
        lane = lax.broadcasted_iota(jnp.int32, (capacity, 128), 1)
        table = jnp.zeros((capacity, 128), jnp.float32)
        for i in range(n_blk):
            hit = row == turned[:, i : i + 1]
            picked = jnp.dot(
                jnp.where(hit, 1.0, 0.0).astype(jnp.bfloat16), x_ref[i], preferred_element_type=jnp.float32
            )
            centre = c_ref[i * capacity : (i + 1) * capacity, :].astype(jnp.float32)
            score = jnp.sum(picked * centre, axis=1, keepdims=True) * scaling
            dual = jnp.where(hit, d_ref[:, i * tok : (i + 1) * tok], 0.0)
            dual = jnp.sum(dual, axis=1, keepdims=True)
            table = jnp.where(lane == i, score + dual, table)
        table = jnp.transpose(table)
        for i in range(n_blk):
            out_ref[:, i * capacity : (i + 1) * capacity] = table[i : i + 1, :]

    return pl.pallas_call(
        kernel,
        out_shape=jax.ShapeDtypeStruct((1, n_blk * capacity), jnp.float32),
        in_specs=vmem(4),
        out_specs=pl.BlockSpec(memory_space=pltpu.VMEM),
        scratch_shapes=[pltpu.VMEM((n_blk, 128), jnp.float32)],
        compiler_params=params(4),
        name="ask_scores",
    )(x, centres, parts, duals)


def look_up(masses, ids, centres, sums, all_rows, n_blk, capacity):
    lines = masses.shape[0]
    slots = n_blk * capacity

    def kernel(m_ref, i_ref, c_ref, s_ref, dual_ref, out_ref):
        dual = math.log(all_rows) - jnp.log(m_ref[...])
        dual_ref[...] = dual
        line = lax.broadcasted_iota(jnp.int32, (lines, slots), 0)
        pick = jnp.where(line == i_ref[0:1, :], 1.0, 0.0).astype(jnp.bfloat16)
        lane = lax.broadcasted_iota(jnp.int32, (128, slots), 0)
        here = lane == i_ref[1:2, :]
        total = jnp.zeros((128, slots), jnp.float32)
        for piece in pieces_of(dual):
            total = total + lax.dot_general(
                piece, pick, (((0,), (0,)), ((), ())), preferred_element_type=jnp.float32
            )
        total = jnp.sum(jnp.where(here, total, 0.0), axis=0, keepdims=True) + s_ref[...]
        pieces = [piece.astype(jnp.float32) for piece in pieces_of(total)]
        blank = jnp.zeros((1, 128 - 3 * capacity), jnp.float32)
        for i in range(n_blk):
            part = slice(i * capacity, (i + 1) * capacity)
            out_ref[i, :capacity, :] = c_ref[part, :]
            row = jnp.concatenate([piece[:, part] for piece in pieces] + [blank], axis=1)
            out_ref[i, capacity:, :] = row.astype(jnp.bfloat16)

    return pl.pallas_call(
        kernel,
        out_shape=(
            jax.ShapeDtypeStruct((lines, 128), jnp.float32),
            jax.ShapeDtypeStruct((n_blk, capacity + 1, 128), jnp.bfloat16),
        ),
        in_specs=vmem(4),
        out_specs=tuple(vmem(2)),
        compiler_params=params(4),
        name="look_up",
    )(masses, ids, centres, sums)


def prepare(tokens, row_ids, counts):
    n_blk, capacity = row_ids.shape
    slots = n_blk * capacity
    tok, width = tokens.shape

    def kernel(n_ref, t_ref, r_ref, row_ref, live_ref, w_ref):
        w_ref[...] = jnp.zeros_like(w_ref)
        w_ref[:, :capacity] = r_ref[...].astype(jnp.float32)
        turned = jnp.transpose(w_ref[...])
        row = lax.broadcasted_iota(jnp.int32, (capacity, tok), 1).astype(jnp.float32)
        place = lax.broadcasted_iota(jnp.int32, (1, 128), 1)
        rows = t_ref[...]
        for i in range(n_blk):
            part = slice(i * capacity, (i + 1) * capacity)
            hit = row == turned[:capacity, i : i + 1]
            row_ref[part, :] = jnp.dot(
                jnp.where(hit, 1.0, 0.0).astype(jnp.bfloat16), rows, preferred_element_type=jnp.float32
            )
            live_ref[i : i + 1, :] = jnp.where(place < n_ref[0, i], 1.0, 0.0)

    return pl.pallas_call(
        kernel,
        out_shape=(
            jax.ShapeDtypeStruct((slots, width), jnp.float32),
            jax.ShapeDtypeStruct((n_blk, 128), jnp.float32),
        ),
        in_specs=[pl.BlockSpec(memory_space=pltpu.SMEM)] + vmem(2),
        out_specs=tuple(vmem(2)),
        scratch_shapes=[pltpu.VMEM((n_blk, 128), jnp.float32)],
        compiler_params=params(4),
        name="prepare",
    )(counts, tokens, row_ids)


def finish(answers, rows, live):
    n_blk, _, width = answers.shape
    capacity = rows.shape[0] // n_blk

    def kernel(g_ref, t_ref, v_ref, out_ref, w_ref):
        for i in range(n_blk):
            w_ref[i : i + 1, :] = g_ref[i, capacity:, :].astype(jnp.float32)
        pieces = w_ref[...]
        exponent = pieces[:, :capacity]
        for k in range(1, 3):
            exponent = exponent + pieces[:, k * capacity : (k + 1) * capacity]
        w_ref[:, :capacity] = jnp.where(v_ref[:, :capacity] > 0.0, jnp.exp(exponent), 0.0)
        turned = jnp.transpose(w_ref[...])
        for i in range(n_blk):
            part = slice(i * capacity, (i + 1) * capacity)
            centre = g_ref[i, :capacity, :].astype(jnp.float32)
            out_ref[0, i] = turned[:capacity, i : i + 1] * (t_ref[part, :] - centre)

    return pl.pallas_call(
        kernel,
        out_shape=jax.ShapeDtypeStruct((1, n_blk, capacity, width), jnp.float32),
        in_specs=vmem(3),
        out_specs=pl.BlockSpec(memory_space=pltpu.VMEM),
        scratch_shapes=[pltpu.VMEM((n_blk, 128), jnp.float32)],
        compiler_params=params(4),
        name="finish",
    )(answers, rows, live)


def local(tokens, centroids, row_ids, alt_ids, counts):
    tok, width = tokens.shape
    slab = centroids.shape[0]
    n_blk = lax.axis_size("blk")
    n_wide = lax.axis_size("wide")
    scaling = score_gain / math.sqrt(width)
    capacity = alt_ids.shape[2]
    pairs = [[k, k + 1] for k in range(0, n_wide, 2)]
    same_core = [list(range(core, n_wide, 2)) for core in range(2)]

    gathered = exchange(stage(tokens, centroids, n_blk), "blk")
    sent, kept, base = row_pass(gathered, centroids, alt_ids[0], row_ids[0], tok, scaling)
    parts = exchange(sent, "blk")
    own_duals, duals, mass = column_pass(gathered, centroids, parts, kept, base, tok, scaling, slab * n_blk)
    both = lax.all_gather(mass, "wide", axis=0, axis_index_groups=pairs, tiled=True)
    mass = add_up(exchange(spread(both, n_wide // 2), "wide", same_core))
    ids = unpack(parts, n_blk * tok, capacity)
    centres = centroids[ids[2]]
    sums = ask_scores(gathered, centres, parts, duals, scaling)
    rows, live = prepare(tokens, row_ids[0], counts)
    mass, sums, rows, live = lax.optimization_barrier((mass, sums, rows, live))
    mass = lax.all_gather(mass, "wide", axis=0, axis_index_groups=pairs, tiled=True)
    col_duals, answers = look_up(mass, ids, centres, sums, tok * n_blk * n_wide, n_blk, capacity)
    residuals = finish(exchange(answers, "blk"), rows, live)
    return (own_duals.reshape(tok), col_duals.reshape(slab), residuals)


def solution(mesh):
    in_specs = (
        P(("blk", "wide"), None),
        P("blk", None),
        P(("blk", "wide"), None, None),
        P(("blk", "wide"), None, None),
        P(("blk", "wide"), None),
    )
    out_specs = (P(("blk", "wide")), P("blk"), P(("blk", "wide"), None, None, None))
    return jax.shard_map(local, mesh=mesh, in_specs=in_specs, out_specs=out_specs, check_vma=False)
```
